512 devices in a mesh: dp: 2 (over core), seq: 64 (over y, z), tensor: 4 (over x).
Axes of the slice: x: 4, y: 8, z: 8, core: 2. Of those that a mesh axis runs over, the one named last changes fastest.
Arguments:
- query: bfloat16 [2, 16384, 2048], P('dp', 'seq', 'tensor'), may hold values from -1.75 to 1.75
- key_rows: bfloat16 [2, 16384, 2048], P('dp', 'seq', 'tensor'), may hold values from -1.75 to 1.75
- value: bfloat16 [2, 16384, 2048], P('dp', 'seq', 'tensor'), may hold values from -40 to 40
- gain: float32 [2048], P('tensor'), may hold values from 0.25 to 1.75
- grad_out: bfloat16 [2, 16384, 2048], P('dp', 'seq', 'tensor'), may hold values from -16 to 16
- start_offset: int32 [2, 256], P('dp', 'seq'), may hold values from 0 to 64, as said below
Outputs:
- attn_out: bfloat16 [2, 16384, 2048], P('dp', 'seq', 'tensor')
- grad_query: bfloat16 [2, 16384, 2048], P('dp', 'seq', 'tensor')
- grad_key: bfloat16 [2, 16384, 2048], P('dp', 'seq', 'tensor')
- grad_value: bfloat16 [2, 16384, 2048], P('dp', 'seq', 'tensor')
- grad_gain: float32 [2048], P('tensor')
The draws below stay inside these ranges and needn't reach their ends.
Inputs may be any that keep to these rules, and one draw needn't show every extreme that they name: `start_offset`: the position within its block of 64 positions at which a document starts; 64 when none starts in the block; every sequence begins a document at its first position.
All inputs are finite; a program needn't handle non-finite values.
Results may differ from the reference program's by a relative error of at most 0.0058.
Values sent between devices are 32-bit elements; how exact they have to be, the bound alone decides.
No kernel may reach another device: no remote copies, remote signals or barrier semaphores. Data moves between devices by JAX's collectives and lax.ppermute only.
A program may use at most 64 MiB of HBM per device.

```python
import jax
import jax.numpy as jnp
from jax import lax

H = 16
DH = 128
TOK_DEV = 256
BLOCKS_DEV = 4
SEQS = 2
LENGTH = 16384
BLOCKS = 256
BLK = 64
CH = 2048
N_SEQ = 64


def draw_value(key, part):
    first, second = jax.random.split(key, 2)
    ladder = jnp.arange(H, dtype=jnp.float32) / (H - 1)
    jitter = jax.random.uniform(second, (H,), minval=0.0, maxval=1.0)
    scales = jnp.exp(jnp.log(3.0) * ladder + jnp.log(3.3) * jitter)
    base = jnp.clip(jax.random.normal(first, (SEQS, LENGTH, CH)), -4.0, 4.0)
    columns = jnp.repeat(scales, DH)
    return (base * columns[None, None, :]).astype(jnp.bfloat16)


def draw_grad_out(key, part):
    ramp = jnp.arange(LENGTH, dtype=jnp.float32) / (LENGTH - 1)
    rows = jnp.exp(jnp.log(3.0) * ramp)
    base = jnp.clip(jax.random.normal(key, (SEQS, LENGTH, CH)), -4.0, 4.0)
    return (base * rows[None, :, None]).astype(jnp.bfloat16)


def draw_start_offset(key, part):
    first, second, third = jax.random.split(key, 3)
    pick = jax.random.randint(first, (SEQS, BLOCKS), 0, 8)
    places = jax.random.randint(second, (SEQS, BLOCKS), 0, BLK)
    offsets = jnp.where(pick == 0, places, BLK)
    windows = BLOCKS // BLOCKS_DEV
    run_windows = 3 * windows // 4
    begin = jax.random.randint(third, (), 1, windows - run_windows + 1)
    window_of = jnp.arange(BLOCKS, dtype=jnp.int32) // BLOCKS_DEV
    inside = (window_of >= begin) & (window_of < begin + run_windows)
    last_row = jnp.arange(SEQS, dtype=jnp.int32) == SEQS - 1
    offsets = jnp.where(last_row[:, None] & inside[None, :], BLK, offsets)
    first_block = jnp.arange(BLOCKS, dtype=jnp.int32) == 0
    offsets = jnp.where(first_block[None, :], 0, offsets)
    return offsets.astype(jnp.int32)


def steps_of(stream_key, shape, cuts, smallest, top_value):
    level, own = 1.0, jax.random.fold_in(stream_key, 6)
    for axis_at, blocks in cuts:
        steps = jnp.exp(jax.random.uniform(jax.random.fold_in(own, axis_at), (blocks,), jnp.float32, smallest / len(cuts), top_value / len(cuts)))
        level = level * jnp.repeat(steps, shape[axis_at] // blocks).reshape([-1 if axis == axis_at else 1 for axis in range(len(shape))])
    return level


def noise(key, extent, spread, most, pieces=(), held_as=jnp.bfloat16):
    result = jax.random.normal(key, extent, jnp.float32) * spread
    if len(pieces) > 0:
        result = steps_of(key, extent, pieces, -0.22, 0.18) * result
    return jnp.clip(result, min=-most, max=most).astype(held_as)


def setup_inputs(seed: int = 0) -> dict:
    keys = jax.random.split(jax.random.key(seed), 7)
    query = noise(keys[0], (SEQS, LENGTH, CH), 0.3, 1.75, ((0, 2), (1, 64), (2, 4)))
    key_rows = noise(keys[1], (SEQS, LENGTH, CH), 0.3, 1.75, ((0, 2), (1, 64), (2, 4)))
    value = draw_value(jax.random.fold_in(keys[6], 71), 0)
    gain = jnp.clip(1.0 + 0.15 * jax.random.normal(keys[3], (CH,), jnp.float32), 0.25, 1.75)
    grad_out = draw_grad_out(jax.random.fold_in(keys[6], 71), 0)
    start_offset = draw_start_offset(jax.random.fold_in(keys[6], 71), 0)
    return dict(query=query, key_rows=key_rows, value=value, gain=gain, grad_out=grad_out, start_offset=start_offset)


eps_value = 1e-05

def segment_rows(offsets, length_dev):
    positions = jnp.arange(length_dev, dtype=jnp.int32)
    block_starts = jnp.arange(offsets.shape[0], dtype=jnp.int32) * BLK + offsets
    present = offsets < BLK
    covered = (block_starts[None, :] <= positions[:, None]) & present[None, :]
    labels = lax.optimization_barrier(jnp.sum(covered.astype(jnp.int32), axis=1))
    allowed = (labels[:, None] == labels[None, :]) & (positions[None, :] <= positions[:, None])
    starts = jnp.sum(present.astype(jnp.int32))
    return (labels, starts, allowed)

def rounded(values):
    return lax.optimization_barrier(values.astype(jnp.bfloat16)).astype(jnp.float32)

def widened(values):
    return values.astype(jnp.float32)

def prefix_step(carry, item):
    part, flag = item
    return (jnp.where(flag > 0, part, carry + part), carry)

def run_prefix(parts, flags, backward):
    start_state = jnp.zeros((H, DH, DH), jnp.float32)
    final_state, outputs = lax.scan(prefix_step, start_state, (parts, flags), reverse=backward)
    return outputs

def reference(query, key_rows, value, gain, grad_out, start_offset):
    blocks_all = SEQS * N_SEQ
    query_blocks = query.reshape(blocks_all, TOK_DEV, H, DH)
    key_blocks = key_rows.reshape(blocks_all, TOK_DEV, H, DH)
    value_blocks = value.reshape(blocks_all, TOK_DEV, H, DH)
    grad_blocks = grad_out.reshape(blocks_all, TOK_DEV, CH)
    offset_blocks = start_offset.reshape(blocks_all, BLOCKS_DEV)

    def forward_block(items):
        query_one, key_one, value_one, offsets = items
        labels, starts, allowed = segment_rows(offsets, TOK_DEV)
        scores = jnp.einsum('thd,shd->hts', widened(query_one), widened(key_one))
        weights = rounded(jnp.where(allowed[None], scores, 0.0))
        local_out = jnp.einsum('hts,shd->thd', weights, widened(value_one))
        tail_keys = jnp.where((labels == starts)[:, None, None], widened(key_one), 0.0)
        tail_state = jnp.einsum('shi,shj->hij', tail_keys, widened(value_one))
        return (local_out, tail_state, (starts > 0).astype(jnp.int32))
    local_out, tail_state, reset = lax.map(forward_block, (query_blocks, key_blocks, value_blocks, offset_blocks))
    tails = tail_state.reshape(SEQS, N_SEQ, H, DH, DH)
    resets = reset.reshape(SEQS, N_SEQ)
    incoming = jnp.stack([run_prefix(tails[index], resets[index], False) for index in range(SEQS)])
    incoming = incoming.reshape(blocks_all, H, DH, DH)

    def middle_block(items):
        query_one, local_one, incoming_one, grad_one, offsets = items
        labels, starts, allowed = segment_rows(offsets, TOK_DEV)
        carried = rounded(incoming_one)
        head_query = jnp.where((labels == 0)[:, None, None], widened(query_one), 0.0)
        carried_out = jnp.einsum('thi,hij->thj', head_query, carried)
        attended = (local_one + carried_out).reshape(TOK_DEV, CH)
        inverse = lax.rsqrt(lax.optimization_barrier(jnp.sum(attended * attended, axis=1)) / CH + eps_value)
        normed = attended * inverse[:, None]
        upstream = widened(grad_one)
        scaled = gain[None, :] * upstream
        output = (gain[None, :] * normed).astype(jnp.bfloat16)
        product_total = lax.optimization_barrier(jnp.sum(scaled * normed, axis=1))
        grad_wide = rounded(inverse[:, None] * (scaled - normed * (product_total / CH)[:, None]))
        gain_part = lax.optimization_barrier(jnp.sum(upstream * normed, axis=0))
        grad_state = jnp.einsum('thi,thj->hij', head_query, grad_wide.reshape(TOK_DEV, H, DH))
        return (output, grad_wide, gain_part, grad_state)
    output, grad_wide, gain_parts, grad_state = lax.map(middle_block, (query_blocks, local_out, incoming, grad_blocks, offset_blocks))
    states = grad_state.reshape(SEQS, N_SEQ, H, DH, DH)
    later = jnp.stack([run_prefix(states[index], resets[index], True) for index in range(SEQS)])
    later = later.reshape(blocks_all, H, DH, DH)

    def backward_block(items):
        query_one, key_one, value_one, grad_one, incoming_one, later_one, offsets = items
        labels, starts, allowed = segment_rows(offsets, TOK_DEV)
        query_wide = widened(query_one)
        key_wide = widened(key_one)
        value_wide = widened(value_one)
        grad_heads = grad_one.reshape(TOK_DEV, H, DH)
        scores = jnp.einsum('thd,shd->hts', query_wide, key_wide)
        weights = rounded(jnp.where(allowed[None], scores, 0.0))
        grad_scores = jnp.einsum('thd,shd->hts', grad_heads, value_wide)
        grad_weights = rounded(jnp.where(allowed[None], grad_scores, 0.0))
        head_mask = (labels == 0)[:, None, None]
        tail_mask = (labels == starts)[:, None, None]
        carried = rounded(incoming_one)
        later_half = rounded(later_one)
        head_grad = jnp.where(head_mask, grad_heads, 0.0)
        tail_keys = jnp.where(tail_mask, key_wide, 0.0)
        tail_values = jnp.where(tail_mask, value_wide, 0.0)
        grad_query = jnp.einsum('hts,shd->thd', grad_weights, key_wide) + jnp.einsum('thj,hij->thi', head_grad, carried)
        grad_key = jnp.einsum('hts,thd->shd', grad_weights, query_wide) + jnp.einsum('shj,hij->shi', tail_values, later_half)
        grad_value = jnp.einsum('hts,thd->shd', weights, grad_heads) + jnp.einsum('shi,hij->shj', tail_keys, later_half)
        return (grad_query.reshape(TOK_DEV, CH).astype(jnp.bfloat16), grad_key.reshape(TOK_DEV, CH).astype(jnp.bfloat16), grad_value.reshape(TOK_DEV, CH).astype(jnp.bfloat16))
    grad_query, grad_key, grad_value = lax.map(backward_block, (query_blocks, key_blocks, value_blocks, grad_wide, incoming, later, offset_blocks))
    shape_all = (SEQS, LENGTH, CH)
    grad_gain = lax.optimization_barrier(jnp.sum(gain_parts, axis=0))
    return (output.reshape(shape_all), grad_query.reshape(shape_all), grad_key.reshape(shape_all), grad_value.reshape(shape_all), grad_gain)
```

```python
import jax
import jax.numpy as jnp
from jax import lax
from jax.experimental import pallas as pl
from jax.experimental.pallas import tpu as pltpu
from jax.sharding import PartitionSpec as P

DH = 128
BLK = 64
CH = 2048
EPS = 1e-05
VMEM = pl.BlockSpec(memory_space=pltpu.VMEM)
SMEM = pl.BlockSpec(memory_space=pltpu.SMEM)
F32 = jnp.float32
BF16 = jnp.bfloat16


def dot(a, b, ca, cb):
    return lax.dot_general(a, b, (((ca,), (cb,)), ((), ())), preferred_element_type=F32)


def bounds(off_ref):
    first, last, count = jnp.int32(1 << 20), jnp.int32(-1), jnp.int32(0)
    for b in range(off_ref.shape[1]):
        off = off_ref[0, b]
        present = off < BLK
        first = jnp.minimum(first, jnp.where(present, b * BLK + off, 1 << 20))
        last = jnp.maximum(last, jnp.where(present, b * BLK + off, -1))
        count += present.astype(jnp.int32)
    return first, last, count


def labels_of(off_ref, pos):
    labels = jnp.zeros(pos.shape, jnp.int32)
    for b in range(off_ref.shape[1]):
        off = off_ref[0, b]
        start = jnp.where(off < BLK, b * BLK + off, 1 << 20)
        labels += (pos >= start).astype(jnp.int32)
    return labels


def allowed_of(off_ref, length):
    t = lax.broadcasted_iota(jnp.int32, (length, length), 0)
    s = lax.broadcasted_iota(jnp.int32, (length, length), 1)
    rows = labels_of(off_ref, lax.broadcasted_iota(jnp.int32, (length, 1), 0))
    cols = labels_of(off_ref, lax.broadcasted_iota(jnp.int32, (1, length), 1))
    return (rows == cols) & (s <= t)


def row_mask(length, first=None, last=None):
    pos = lax.broadcasted_iota(jnp.int32, (length, DH), 0)
    return pos < first if last is None else pos >= last


def put_slices(send_ref, h, state):
    for j in range(DH // 8):
        at = 9 * (h * (DH // 8) + j)
        send_ref[at : at + 8, :] = state[8 * j : 8 * j + 8, :]


def head(h):
    return slice(h * DH, (h + 1) * DH)


def tail_kernel(off_ref, k_ref, v_ref, send_ref):
    length, width = k_ref.shape
    _, last, count = bounds(off_ref)
    tail = row_mask(length, last=last)
    for h in range(width // DH):
        keys = jnp.where(tail, k_ref[:, head(h)], jnp.zeros((), BF16))
        put_slices(send_ref, h, dot(keys, v_ref[:, head(h)], 0, 0))
    keep = jnp.full((1, DH), jnp.where(count > 0, 0.0, 1.0), F32)
    for j in range(send_ref.shape[0] // 9):
        send_ref[9 * j + 8 : 9 * j + 9, :] = keep


def local_kernel(off_ref, q_ref, k_ref, v_ref, out_ref):
    length, width = q_ref.shape
    allowed = allowed_of(off_ref, length)
    for h in range(width // DH):
        scores = dot(q_ref[:, head(h)], k_ref[:, head(h)], 1, 1)
        weights = jnp.where(allowed, scores, 0.0).astype(BF16)
        out_ref[:, head(h)] = dot(weights, v_ref[:, head(h)], 1, 0)


def prefix_kernel(recv_ref, send_ref):
    carry = jnp.zeros((8, DH), F32)
    for w in range(recv_ref.shape[0] // 9):
        send_ref[8 * w : 8 * w + 8, :] = carry
        keep = jnp.broadcast_to(recv_ref[9 * w + 8 : 9 * w + 9, :], (8, DH))
        carry = recv_ref[9 * w : 9 * w + 8, :] + carry * keep


def attend_kernel(off_ref, q_ref, local_ref, state_ref, g_ref, gain_ref, att_ref, sums_ref):
    length, width = q_ref.shape
    first, _, _ = bounds(off_ref)
    opened = row_mask(length, first=first)
    squares = jnp.zeros((length, DH), F32)
    products = jnp.zeros((length, DH), F32)
    for h in range(width // DH):
        query = jnp.where(opened, q_ref[:, head(h)], jnp.zeros((), BF16))
        carried = state_ref[h * DH : (h + 1) * DH, :].astype(BF16)
        att = local_ref[:, head(h)] + dot(query, carried, 1, 0)
        att_ref[:, head(h)] = att
        squares += att * att
        products += (gain_ref[:, head(h)] * g_ref[:, head(h)].astype(F32)) * att
    row = 0
    for total in (squares, products):
        for half in range(length // DH):
            line = jnp.sum(total[half * DH : (half + 1) * DH, :].T, axis=0, keepdims=True)
            for c in range(4):
                sums_ref[4 * c + row : 4 * c + row + 1, :] = line
            row += 1


def norm_kernel(off_ref, q_ref, att_ref, g_ref, gain_ref, sums_ref, out_ref, pre_ref, send_ref):
    length, width = q_ref.shape
    first, _, _ = bounds(off_ref)
    opened = row_mask(length, first=first)
    total = sums_ref[0:4, :] + sums_ref[4:8, :] + sums_ref[8:12, :] + sums_ref[12:16, :]
    halves = length // DH
    inverses, means = [], []
    for half in range(halves):
        inv = lax.rsqrt(total[half : half + 1, :] / CH + EPS)
        mean = inv * total[halves + half : halves + half + 1, :] / CH
        inverses.append(jnp.broadcast_to(inv, (DH, DH)).T)
        means.append(jnp.broadcast_to(mean, (DH, DH)).T)
    inverse = jnp.concatenate(inverses, axis=0)
    mean = jnp.concatenate(means, axis=0)
    zero = jnp.zeros((1, DH), F32)
    for j in range(width // DH, send_ref.shape[0] // 9):
        send_ref[9 * j + 8 : 9 * j + 9, :] = zero
    for h in range(width // DH):
        upstream = g_ref[:, head(h)].astype(F32)
        gain = gain_ref[:, head(h)]
        normed = att_ref[:, head(h)] * inverse
        out_ref[:, head(h)] = (gain * normed).astype(BF16)
        pre = (inverse * (gain * upstream - normed * mean)).astype(BF16)
        pre_ref[:, head(h)] = pre
        send_ref[9 * h + 8 : 9 * h + 9, :] = jnp.sum(upstream * normed, axis=0, keepdims=True)
        query = jnp.where(opened, q_ref[:, head(h)], jnp.zeros((), BF16))
        put_slices(send_ref, h, dot(query, pre, 0, 0))


def suffix_kernel(flags_ref, recv_ref, send_ref):
    count = recv_ref.shape[0] // 9
    carry = jnp.zeros((8, DH), F32)
    total = jnp.zeros((1, DH), F32)
    for w in reversed(range(count)):
        send_ref[9 * w : 9 * w + 8, :] = carry
        keep = jnp.broadcast_to(flags_ref[9 * w + 8 : 9 * w + 9, :], (8, DH))
        carry = recv_ref[9 * w : 9 * w + 8, :] + carry * keep
        total += recv_ref[9 * w + 8 : 9 * w + 9, :]
    for w in range(count):
        send_ref[9 * w + 8 : 9 * w + 9, :] = total


def grads_kernel(off_ref, q_ref, k_ref, v_ref, pre_ref, state_ref, gq_ref, gk_ref, gv_ref):
    length, width = q_ref.shape
    first, _, _ = bounds(off_ref)
    opened = row_mask(length, first=first)
    allowed = allowed_of(off_ref, length)
    for h in range(width // DH):
        query, key, value, pre = (r[:, head(h)] for r in (q_ref, k_ref, v_ref, pre_ref))
        scores = dot(query, key, 1, 1)
        weights = jnp.where(allowed, scores, 0.0).astype(BF16)
        gv_ref[:, head(h)] = dot(weights, pre, 0, 0)
        grad_scores = dot(pre, value, 1, 1)
        grad_weights = jnp.where(allowed, grad_scores, 0.0).astype(BF16)
        gk_ref[:, head(h)] = dot(grad_weights, query, 0, 0)
        carried = state_ref[h * DH : (h + 1) * DH, :].astype(BF16)
        head_pre = jnp.where(opened, pre, jnp.zeros((), BF16))
        gq_ref[:, head(h)] = (
            dot(grad_weights, key, 1, 0) + dot(head_pre, carried, 1, 1)
        ).astype(BF16)


def final_kernel(off_ref, k_ref, v_ref, recv_ref, gk_ref, gv_ref, outk_ref, outv_ref, gain_ref):
    length, width = k_ref.shape
    _, last, _ = bounds(off_ref)
    tail = row_mask(length, last=last)
    for h in range(width // DH):
        rows = [9 * (h * (DH // 8) + j) for j in range(DH // 8)]
        later = jnp.concatenate([recv_ref[r : r + 8, :] for r in rows], axis=0).astype(BF16)
        keys = jnp.where(tail, k_ref[:, head(h)], jnp.zeros((), BF16))
        values = jnp.where(tail, v_ref[:, head(h)], jnp.zeros((), BF16))
        outk_ref[:, head(h)] = (gk_ref[:, head(h)] + dot(values, later, 1, 1)).astype(BF16)
        outv_ref[:, head(h)] = (gv_ref[:, head(h)] + dot(keys, later, 1, 0)).astype(BF16)
        gain_ref[h : h + 1, :] = recv_ref[9 * h + 8 : 9 * h + 9, :]


def call(kernel, outs, flops, bytes_accessed, *args):
    return pl.pallas_call(
        kernel,
        out_shape=[jax.ShapeDtypeStruct(s, d) for s, d in outs],
        in_specs=[SMEM if a.dtype == jnp.int32 else VMEM for a in args],
        out_specs=[VMEM] * len(outs),
        cost_estimate=pl.CostEstimate(
            flops=flops, bytes_accessed=bytes_accessed, transcendentals=0
        ),
    )(*args)


def exchanged(rows, per):
    count = rows.shape[0] // per
    shape = (count, per, DH) if per == 8 else (count, per, 1, DH)
    return lax.all_to_all(rows.reshape(shape), "seq", 0, 0).reshape(rows.shape)


def shards(query, key_rows, value, gain, grad_out, start_offset):
    q, k, v, g = query[0], key_rows[0], value[0], grad_out[0]
    length, width = q.shape
    off = start_offset
    gain = gain.reshape(1, width)
    count = lax.axis_size("seq")
    wide = (length, width)
    mega = 1 << 20
    (tails,) = call(tail_kernel, [((count * 9, DH), F32)], 34 * mega, mega, off, k, v)
    tails = exchanged(tails, 9)
    (local,) = call(local_kernel, [(wide, F32)], 134 * mega, mega, off, q, k, v)
    (prefixes,) = call(prefix_kernel, [((count * 8, DH), F32)], mega, mega, tails)
    state = exchanged(prefixes, 8)
    att, sums = call(
        attend_kernel, [(wide, F32), ((16, DH), F32)], 34 * mega, mega, off, q, local, state, g, gain
    )
    sums = lax.all_to_all(sums.reshape(4, 4, DH), "tensor", 0, 0).reshape(16, DH)
    out, pre, grad_states = call(
        norm_kernel,
        [(wide, BF16), (wide, BF16), ((count * 9, DH), F32)],
        34 * mega,
        mega,
        off,
        q,
        att,
        g,
        gain,
        sums,
    )
    grad_states = exchanged(grad_states, 9)
    gq, gk, gv = call(
        grads_kernel,
        [(wide, BF16), (wide, F32), (wide, F32)],
        340 * mega,
        3 * mega,
        off,
        q,
        k,
        v,
        pre,
        state,
    )
    (suffixes,) = call(suffix_kernel, [((count * 9, DH), F32)], mega, mega, tails, grad_states)
    later = exchanged(suffixes, 9)
    gk, gv, gain_sum = call(
        final_kernel,
        [(wide, BF16), (wide, BF16), ((width // DH, DH), F32)],
        68 * mega,
        2 * mega,
        off,
        k,
        v,
        later,
        gk,
        gv,
    )
    grad_gain = lax.psum(gain_sum, "dp").reshape(width)
    return out[None], gq[None], gk[None], gv[None], grad_gain


def solution(mesh):
    wide = P("dp", "seq", "tensor")
    return jax.shard_map(
        shards,
        mesh=mesh,
        in_specs=(wide, wide, wide, P("tensor"), wide, P("dp", "seq")),
        out_specs=(wide, wide, wide, wide, P("tensor")),
        check_vma=False,
    )
```

```python
import jax
import jax.numpy as jnp
from jax import lax
from jax.experimental import pallas as pl
from jax.experimental.pallas import tpu as pltpu
from jax.sharding import PartitionSpec as P

DH = 128
BLK = 64
CH = 2048
EPS = 1e-05
ROOT = 36
VMEM = pl.BlockSpec(memory_space=pltpu.VMEM)
SMEM = pl.BlockSpec(memory_space=pltpu.SMEM)
HBM = pl.BlockSpec(memory_space=pltpu.HBM)
F32 = jnp.float32
BF16 = jnp.bfloat16


def dot(a, b, ca, cb):
    return lax.dot_general(a, b, (((ca,), (cb,)), ((), ())), preferred_element_type=F32)


def bounds(off_ref):
    first, last, count = jnp.int32(1 << 20), jnp.int32(-1), jnp.int32(0)
    for b in range(off_ref.shape[1]):
        off = off_ref[0, b]
        present = off < BLK
        first = jnp.minimum(first, jnp.where(present, b * BLK + off, 1 << 20))
        last = jnp.maximum(last, jnp.where(present, b * BLK + off, -1))
        count += present.astype(jnp.int32)
    return first, last, count


def labels_of(off_ref, pos):
    labels = jnp.zeros(pos.shape, jnp.int32)
    for b in range(off_ref.shape[1]):
        off = off_ref[0, b]
        start = jnp.where(off < BLK, b * BLK + off, 1 << 20)
        labels += (pos >= start).astype(jnp.int32)
    return labels


def allowed_of(off_ref, length):
    t = lax.broadcasted_iota(jnp.int32, (length, length), 0)
    s = lax.broadcasted_iota(jnp.int32, (length, length), 1)
    rows = labels_of(off_ref, lax.broadcasted_iota(jnp.int32, (length, 1), 0))
    cols = labels_of(off_ref, lax.broadcasted_iota(jnp.int32, (1, length), 1))
    return (rows == cols) & (s <= t)


def row_mask(length, first=None, last=None):
    pos = lax.broadcasted_iota(jnp.int32, (length, DH), 0)
    return pos < first if last is None else pos >= last


def put_slices(send_ref, h, state):
    for j in range(DH // 8):
        at = 9 * (h * (DH // 8) + j)
        send_ref[at : at + 8, :] = state[8 * j : 8 * j + 8, :]


def head(h):
    return slice(h * DH, (h + 1) * DH)


def tail_kernel(off_hbm, k_hbm, v_hbm, send_hbm, off_ref, k_ref, v_ref, send_ref, sems, sent):
    copies = [
        pltpu.make_async_copy(source, target, sems.at[i])
        for i, (source, target) in enumerate(
            ((off_hbm, off_ref), (k_hbm, k_ref), (v_hbm, v_ref))
        )
    ]
    for copy in copies:
        copy.start()
    length, width = k_ref.shape
    copies[0].wait()
    _, last, count = bounds(off_ref)
    tail = row_mask(length, last=last)
    keep = jnp.full((1, DH), jnp.where(count > 0, 0.0, 1.0), F32)
    for j in range(send_ref.shape[0] // 9):
        send_ref[9 * j + 8 : 9 * j + 9, :] = keep
    copies[1].wait()
    copies[2].wait()
    outs = []
    for h in range(width // DH):
        keys = jnp.where(tail, k_ref[:, head(h)], jnp.zeros((), BF16))
        put_slices(send_ref, h, dot(keys, v_ref[:, head(h)], 0, 0))
        rows = slice(h * 9 * (DH // 8), (h + 1) * 9 * (DH // 8))
        outs.append(pltpu.make_async_copy(send_ref.at[rows], send_hbm.at[rows], sent.at[h]))
        outs[-1].start()
    for copy in outs:
        copy.wait()


def local_kernel(off_ref, q_ref, k_ref, v_ref, g_ref, gain_ref, out_ref, scaled_ref, token_ref):
    length, width = q_ref.shape
    allowed = allowed_of(off_ref, length)
    for h in range(width // DH):
        scores = dot(q_ref[:, head(h)], k_ref[:, head(h)], 1, 1)
        weights = jnp.where(allowed, scores, 0.0).astype(BF16)
        out_ref[:, head(h)] = dot(weights, v_ref[:, head(h)], 1, 0)
        scaled_ref[:, head(h)] = gain_ref[:, head(h)] * g_ref[:, head(h)].astype(F32)
    token_ref[...] = jnp.zeros_like(token_ref)


def order_of(count):
    side = 8

    def distance(w):
        steps = (abs(w // side - ROOT // side), abs(w % side - ROOT % side))
        return sum(min(d, side - d) for d in steps)

    return [ROOT] + sorted((w for w in range(count) if w != ROOT), key=lambda w: -distance(w))


def slots_of(count):
    order = order_of(count)
    return [order.index(w) for w in range(count)]


def prefix_kernel(recv_ref, token_ref, send_ref):
    carry = token_ref[...]
    for w in slots_of(recv_ref.shape[0] // 9):
        send_ref[8 * w : 8 * w + 8, :] = carry
        keep = jnp.broadcast_to(recv_ref[9 * w + 8 : 9 * w + 9, :], (8, DH))
        carry = recv_ref[9 * w : 9 * w + 8, :] + carry * keep


def attend_kernel(off_ref, q_ref, local_ref, state_ref, scaled_ref, att_ref, sums_ref):
    length, width = q_ref.shape
    first, _, _ = bounds(off_ref)
    opened = row_mask(length, first=first)
    squares = jnp.zeros((length, DH), F32)
    products = jnp.zeros((length, DH), F32)
    for h in range(width // DH):
        carried = state_ref[h * DH : (h + 1) * DH, :].astype(BF16)
        carried_out = dot(q_ref[:, head(h)], carried, 1, 0)
        att = local_ref[:, head(h)] + jnp.where(opened, carried_out, 0.0)
        att_ref[:, head(h)] = att
        squares += att * att
        products += scaled_ref[:, head(h)] * att
    row = 0
    for total in (squares, products):
        for half in range(length // DH):
            line = jnp.sum(total[half * DH : (half + 1) * DH, :].T, axis=0, keepdims=True)
            for c in range(4):
                sums_ref[4 * c + row : 4 * c + row + 1, :] = line
            row += 1


def columns_of(sums_ref, length):
    total = sums_ref[0:4, :] + sums_ref[4:8, :] + sums_ref[8:12, :] + sums_ref[12:16, :]
    halves = length // DH
    inv = lax.rsqrt(total[0:halves, :] / CH + EPS)
    mean = inv * total[halves : 2 * halves, :] / CH
    cols = jnp.concatenate([inv, mean, inv, mean], axis=0).T
    inverse = jnp.concatenate([cols[:, i : i + 1] for i in range(halves)], axis=0)
    mean = jnp.concatenate([cols[:, halves + i : halves + i + 1] for i in range(halves)], axis=0)
    return jnp.broadcast_to(inverse, (length, DH)), jnp.broadcast_to(mean, (length, DH))


def pre_kernel(
    off_ref, q_ref, att_ref, g_ref, scaled_ref, gain_ref, sums_ref,
    pre_ref, out_hbm, send_hbm, out_ref, send_ref, sems,
):
    length, width = q_ref.shape
    first, _, _ = bounds(off_ref)
    opened = row_mask(length, first=first)
    inverse, mean = columns_of(sums_ref, length)
    copies, parts, pres = [], [], []
    for h in range(width // DH):
        normed = att_ref[:, head(h)] * inverse
        out_ref[:, head(h)] = (gain_ref[:, head(h)] * normed).astype(BF16)
        copies.append(
            pltpu.make_async_copy(
                out_ref.at[:, head(h)], out_hbm.at[:, head(h)], sems.at[0, h]
            )
        )
        copies[-1].start()
        pre = inverse * (scaled_ref[:, head(h)] - normed * mean)
        pre_ref[:, head(h)] = pre.astype(BF16)
        pres.append(jnp.where(opened, pre, 0.0).astype(BF16))
        upstream = g_ref[:, head(h)].astype(F32)
        parts.append(jnp.sum(upstream * normed, axis=0, keepdims=True))
    part = jnp.concatenate(parts, axis=0)
    for j in range(send_ref.shape[0] // 12):
        send_ref[12 * j + 8 : 12 * j + 12, :] = part
    for h in range(width // DH):
        state = dot(q_ref[:, head(h)], pres[h], 0, 0)
        for j in range(DH // 8):
            at = 12 * (h * (DH // 8) + j)
            send_ref[at : at + 8, :] = state[8 * j : 8 * j + 8, :]
        rows = slice(h * 12 * (DH // 8), (h + 1) * 12 * (DH // 8))
        copies.append(pltpu.make_async_copy(send_ref.at[rows], send_hbm.at[rows], sems.at[1, h]))
        copies[-1].start()
    for copy in copies:
        copy.wait()


def suffix_kernel(flags_ref, recv_ref, token_ref, send_ref, after_ref):
    carry = token_ref[...]
    after_ref[...] = carry
    for w in reversed(slots_of(recv_ref.shape[0] // 12)):
        send_ref[8 * w : 8 * w + 8, :] = carry
        keep = jnp.broadcast_to(flags_ref[9 * w + 8 : 9 * w + 9, :], (8, DH))
        carry = recv_ref[12 * w : 12 * w + 8, :] + carry * keep


def part_kernel(recv_ref, token_ref, part_ref):
    sums = [token_ref[4 * (i % 2) : 4 * (i % 2) + 4, :] for i in range(4)]
    for w in range(recv_ref.shape[0] // 12):
        sums[w % 4] += recv_ref[12 * w + 8 : 12 * w + 12, :]
    part_ref[...] = (sums[0] + sums[1]) + (sums[2] + sums[3])


def grads_kernel(
    off_ref, q_ref, k_ref, v_ref, pre_ref, state_ref, gq_ref, gk_ref, gv_ref, token_ref
):
    length, width = q_ref.shape
    token_ref[...] = jnp.zeros_like(token_ref)
    first, _, _ = bounds(off_ref)
    opened = row_mask(length, first=first)
    allowed = allowed_of(off_ref, length)
    for h in range(width // DH):
        query, key, value, pre = (r[:, head(h)] for r in (q_ref, k_ref, v_ref, pre_ref))
        scores = dot(query, key, 1, 1)
        weights = jnp.where(allowed, scores, 0.0).astype(BF16)
        gv_ref[:, head(h)] = dot(weights, pre, 0, 0)
        grad_scores = dot(pre, value, 1, 1)
        grad_weights = jnp.where(allowed, grad_scores, 0.0).astype(BF16)
        gk_ref[:, head(h)] = dot(grad_weights, query, 0, 0)
        carried = state_ref[h * DH : (h + 1) * DH, :].astype(BF16)
        carried_grad = jnp.where(opened, dot(pre, carried, 1, 1), 0.0)
        gq_ref[:, head(h)] = (dot(grad_weights, key, 1, 0) + carried_grad).astype(BF16)


def final_kernel(
    off_ref, k_ref, v_ref, later_ref, gk_ref, gv_ref, part_ref, other_ref,
    outk_hbm, outv_hbm, gain_ref, outk, outv, sems,
):
    length, width = k_ref.shape
    _, last, _ = bounds(off_ref)
    tail = row_mask(length, last=last)
    copies = []
    for h in range(width // DH):
        later = later_ref[h * DH : (h + 1) * DH, :].astype(BF16)
        from_values = jnp.where(tail, dot(v_ref[:, head(h)], later, 1, 1), 0.0)
        from_keys = jnp.where(tail, dot(k_ref[:, head(h)], later, 1, 0), 0.0)
        outk[:, head(h)] = (gk_ref[:, head(h)] + from_values).astype(BF16)
        outv[:, head(h)] = (gv_ref[:, head(h)] + from_keys).astype(BF16)
        for i, (source, target) in enumerate(((outk, outk_hbm), (outv, outv_hbm))):
            copies.append(
                pltpu.make_async_copy(
                    source.at[:, head(h)], target.at[:, head(h)], sems.at[i, h]
                )
            )
            copies[-1].start()
    gain_ref[...] = part_ref[...] + other_ref[...]
    for copy in copies:
        copy.wait()


def call(kernel, outs, flops, bytes_accessed, *args, ins=None, out_specs=None, scratch=(), grant=12):
    return pl.pallas_call(
        kernel,
        out_shape=[jax.ShapeDtypeStruct(s, d) for s, d in outs],
        in_specs=ins or [SMEM if a.dtype == jnp.int32 else VMEM for a in args],
        out_specs=out_specs or [VMEM] * len(outs),
        scratch_shapes=list(scratch),
        compiler_params=pltpu.CompilerParams(vmem_limit_bytes=grant << 20),
        cost_estimate=pl.CostEstimate(
            flops=flops, bytes_accessed=bytes_accessed, transcendentals=0
        ),
    )(*args)


def exchanged(rows, per):
    count = rows.shape[0] // per
    tile = {8: (8,), 9: (9, 1), 12: (3, 4)}[per]
    groups = [order_of(count)]
    moved = lax.all_to_all(
        rows.reshape((count, *tile, DH)), "seq", 0, 0, axis_index_groups=groups
    )
    return moved.reshape(rows.shape)


def shards(query, key_rows, value, gain, grad_out, start_offset):
    q, k, v, g = query[0], key_rows[0], value[0], grad_out[0]
    length, width = q.shape
    heads = width // DH
    off = start_offset
    gain = gain.reshape(1, width)
    count = lax.axis_size("seq")
    wide = (length, width)
    mega = 1 << 20
    dma = pltpu.SemaphoreType.DMA
    (tails,) = call(
        tail_kernel,
        [((count * 9, DH), F32)],
        34 * mega,
        mega,
        off,
        k,
        v,
        ins=[HBM] * 3,
        out_specs=[HBM],
        scratch=(
            pltpu.SMEM(off.shape, jnp.int32),
            pltpu.VMEM(wide, BF16),
            pltpu.VMEM(wide, BF16),
            pltpu.VMEM((count * 9, DH), F32),
            dma((3,)),
            dma((heads,)),
        ),
        grant=63,
    )
    tails = exchanged(tails, 9)
    token = (8, DH)
    local, scaled, ready = call(
        local_kernel,
        [(wide, F32), (wide, F32), (token, F32)],
        134 * mega,
        mega,
        off,
        q,
        k,
        v,
        g,
        gain,
    )
    (prefixes,) = call(prefix_kernel, [((count * 8, DH), F32)], mega, mega, tails, ready)
    state = exchanged(prefixes, 8)
    att, sums = call(
        attend_kernel, [(wide, F32), ((16, DH), F32)], 34 * mega, mega, off, q, local, state, scaled
    )
    sums = lax.all_to_all(
        sums.reshape(4, 4, DH), "tensor", 0, 0, axis_index_groups=[[2, 3, 1, 0]]
    ).reshape(16, DH)
    pre, out, grad_states = call(
        pre_kernel,
        [(wide, BF16), (wide, BF16), ((count * 12, DH), F32)],
        34 * mega,
        mega,
        off,
        q,
        att,
        g,
        scaled,
        gain,
        sums,
        out_specs=[VMEM, HBM, HBM],
        scratch=(
            pltpu.VMEM(wide, BF16),
            pltpu.VMEM((count * 12, DH), F32),
            dma((2, heads)),
        ),
    )
    grad_states = exchanged(grad_states, 12)
    gq, gk, gv, ready = call(
        grads_kernel,
        [(wide, BF16), (wide, F32), (wide, F32), (token, F32)],
        340 * mega,
        3 * mega,
        off,
        q,
        k,
        v,
        pre,
        state,
    )
    suffixes, ready = call(
        suffix_kernel,
        [((count * 8, DH), F32), (token, F32)],
        mega,
        mega,
        tails,
        grad_states,
        ready,
    )
    later = exchanged(suffixes, 8)
    (part,) = call(part_kernel, [((heads, DH), F32)], mega, mega, grad_states, ready)
    other = lax.ppermute(part, "dp", [(0, 1), (1, 0)])
    gk, gv, gain_sum = call(
        final_kernel,
        [(wide, BF16), (wide, BF16), ((heads, DH), F32)],
        68 * mega,
        2 * mega,
        off,
        k,
        v,
        later,
        gk,
        gv,
        part,
        other,
        out_specs=[HBM, HBM, VMEM],
        scratch=(pltpu.VMEM(wide, BF16), pltpu.VMEM(wide, BF16), dma((2, heads))),
    )
    return out[None], gq[None], gk[None], gv[None], gain_sum.reshape(width)


def solution(mesh):
    wide = P("dp", "seq", "tensor")
    return jax.shard_map(
        shards,
        mesh=mesh,
        in_specs=(wide, wide, wide, P("tensor"), wide, P("dp", "seq")),
        out_specs=(wide, wide, wide, wide, P("tensor")),
        check_vma=False,
    )
```

```python
import jax
import jax.numpy as jnp
from jax import lax
from jax.experimental import pallas as pl
from jax.experimental.pallas import tpu as pltpu
from jax.sharding import PartitionSpec as P

DH = 128
BLK = 64
CH = 2048
EPS = 1e-05
ROOT = 36
VMEM = pl.BlockSpec(memory_space=pltpu.VMEM)
SMEM = pl.BlockSpec(memory_space=pltpu.SMEM)
HBM = pl.BlockSpec(memory_space=pltpu.HBM)
F32 = jnp.float32
BF16 = jnp.bfloat16


def dot(a, b, ca, cb):
    return lax.dot_general(a, b, (((ca,), (cb,)), ((), ())), preferred_element_type=F32)


def bounds(off_ref):
    first, last, count = jnp.int32(1 << 20), jnp.int32(-1), jnp.int32(0)
    for b in range(off_ref.shape[1]):
        off = off_ref[0, b]
        present = off < BLK
        first = jnp.minimum(first, jnp.where(present, b * BLK + off, 1 << 20))
        last = jnp.maximum(last, jnp.where(present, b * BLK + off, -1))
        count += present.astype(jnp.int32)
    return first, last, count


def labels_of(off_ref, pos):
    labels = jnp.zeros(pos.shape, jnp.int32)
    for b in range(off_ref.shape[1]):
        off = off_ref[0, b]
        start = jnp.where(off < BLK, b * BLK + off, 1 << 20)
        labels += (pos >= start).astype(jnp.int32)
    return labels


def allowed_of(off_ref, length):
    t = lax.broadcasted_iota(jnp.int32, (length, length), 0)
    s = lax.broadcasted_iota(jnp.int32, (length, length), 1)
    rows = labels_of(off_ref, lax.broadcasted_iota(jnp.int32, (length, 1), 0))
    cols = labels_of(off_ref, lax.broadcasted_iota(jnp.int32, (1, length), 1))
    return (rows == cols) & (s <= t)


def row_mask(length, first=None, last=None):
    pos = lax.broadcasted_iota(jnp.int32, (length, DH), 0)
    return pos < first if last is None else pos >= last


def put_slices(send_ref, h, state):
    for j in range(DH // 8):
        at = 9 * (h * (DH // 8) + j)
        send_ref[at : at + 8, :] = state[8 * j : 8 * j + 8, :]


def head(h):
    return slice(h * DH, (h + 1) * DH)


def tail_kernel(off_hbm, k_hbm, v_hbm, send_hbm, off_ref, k_ref, v_ref, send_ref, sems, sent):
    copies = [
        pltpu.make_async_copy(source, target, sems.at[i])
        for i, (source, target) in enumerate(
            ((off_hbm, off_ref), (k_hbm, k_ref), (v_hbm, v_ref))
        )
    ]
    for copy in copies:
        copy.start()
    length, width = k_ref.shape
    copies[0].wait()
    _, last, count = bounds(off_ref)
    tail = row_mask(length, last=last)
    keep = jnp.full((1, DH), jnp.where(count > 0, 0.0, 1.0), F32)
    for j in range(send_ref.shape[0] // 9):
        send_ref[9 * j + 8 : 9 * j + 9, :] = keep
    copies[1].wait()
    copies[2].wait()
    outs = []
    for h in range(width // DH):
        keys = jnp.where(tail, k_ref[:, head(h)], jnp.zeros((), BF16))
        put_slices(send_ref, h, dot(keys, v_ref[:, head(h)], 0, 0))
        rows = slice(h * 9 * (DH // 8), (h + 1) * 9 * (DH // 8))
        outs.append(pltpu.make_async_copy(send_ref.at[rows], send_hbm.at[rows], sent.at[h]))
        outs[-1].start()
    for copy in outs:
        copy.wait()


def local_kernel(off_ref, q_ref, k_ref, v_ref, gain_ref, out_ref, token_ref):
    length, width = q_ref.shape
    allowed = allowed_of(off_ref, length)
    for h in range(width // DH):
        scores = dot(q_ref[:, head(h)], k_ref[:, head(h)], 1, 1)
        weights = jnp.where(allowed, scores, 0.0).astype(BF16)
        out_ref[:, head(h)] = dot(weights, v_ref[:, head(h)], 1, 0)
    token_ref[...] = jnp.zeros_like(token_ref)


def order_of(count):
    side = 8

    def distance(w):
        steps = (abs(w // side - ROOT // side), abs(w % side - ROOT % side))
        return sum(min(d, side - d) for d in steps)

    return [ROOT] + sorted((w for w in range(count) if w != ROOT), key=lambda w: -distance(w))


def slots_of(count):
    order = order_of(count)
    return [order.index(w) for w in range(count)]


def prefix_kernel(recv_ref, token_ref, send_ref, keep_ref):
    carry = token_ref[...]
    for w in slots_of(recv_ref.shape[0] // 9):
        send_ref[8 * w : 8 * w + 8, :] = carry
        flag = recv_ref[9 * w + 8 : 9 * w + 9, :]
        keep_ref[w : w + 1, :] = flag
        carry = recv_ref[9 * w : 9 * w + 8, :] + carry * jnp.broadcast_to(flag, (8, DH))


def attend_kernel(
    off_ref, q_ref, local_ref, state_ref, g_ref, gain_ref, att_ref, sums_ref, carried_ref
):
    length, width = q_ref.shape
    first, _, _ = bounds(off_ref)
    opened = row_mask(length, first=first)
    squares = jnp.zeros((length, DH), F32)
    products = jnp.zeros((length, DH), F32)
    for h in range(width // DH):
        carried = state_ref[h * DH : (h + 1) * DH, :].astype(BF16)
        carried_ref[h * DH : (h + 1) * DH, :] = carried
        carried_out = dot(q_ref[:, head(h)], carried, 1, 0)
        att = local_ref[:, head(h)] + jnp.where(opened, carried_out, 0.0)
        att_ref[:, head(h)] = att
        squares += att * att
        products += (gain_ref[:, head(h)] * g_ref[:, head(h)].astype(F32)) * att
    row = 0
    for total in (squares, products):
        for half in range(length // DH):
            line = jnp.sum(total[half * DH : (half + 1) * DH, :].T, axis=0, keepdims=True)
            for c in range(4):
                sums_ref[4 * c + row : 4 * c + row + 1, :] = line
            row += 1


def columns_of(sums_ref, length):
    total = sums_ref[0:4, :] + sums_ref[4:8, :] + sums_ref[8:12, :] + sums_ref[12:16, :]
    halves = length // DH
    inv = lax.rsqrt(total[0:halves, :] / CH + EPS)
    mean = inv * total[halves : 2 * halves, :] / CH
    cols = jnp.concatenate([inv, mean, inv, mean], axis=0).T
    inverse = jnp.concatenate([cols[:, i : i + 1] for i in range(halves)], axis=0)
    mean = jnp.concatenate([cols[:, halves + i : halves + i + 1] for i in range(halves)], axis=0)
    return jnp.broadcast_to(inverse, (length, DH)), jnp.broadcast_to(mean, (length, DH))


def pre_kernel(off_ref, q_ref, att_ref, g_ref, gain_ref, sums_ref, pre_ref, send_ref):
    length, width = q_ref.shape
    first, _, _ = bounds(off_ref)
    opened = row_mask(length, first=first)
    inverse, mean = columns_of(sums_ref, length)
    parts = []
    for h in range(width // DH):
        normed = att_ref[:, head(h)] * inverse
        upstream = g_ref[:, head(h)].astype(F32)
        pre = inverse * (gain_ref[:, head(h)] * upstream - normed * mean)
        pre_ref[:, head(h)] = pre.astype(BF16)
        state = dot(q_ref[:, head(h)], jnp.where(opened, pre, 0.0).astype(BF16), 0, 0)
        for j in range(DH // 8):
            at = 12 * (h * (DH // 8) + j)
            send_ref[at : at + 8, :] = state[8 * j : 8 * j + 8, :]
        parts.append(jnp.sum(upstream * normed, axis=0, keepdims=True))
    part = jnp.concatenate(parts, axis=0)
    for j in range(send_ref.shape[0] // 12):
        send_ref[12 * j + 8 : 12 * j + 12, :] = part


def suffix_kernel(flags_ref, recv_ref, token_ref, send_ref, after_ref):
    carry = token_ref[...]
    after_ref[...] = carry
    for w in reversed(slots_of(recv_ref.shape[0] // 12)):
        send_ref[8 * w : 8 * w + 8, :] = carry
        keep = jnp.broadcast_to(flags_ref[w : w + 1, :], (8, DH))
        carry = recv_ref[12 * w : 12 * w + 8, :] + carry * keep


def part_kernel(recv_ref, token_ref, part_ref):
    sums = [token_ref[4 * (i % 2) : 4 * (i % 2) + 4, :] for i in range(4)]
    for w in range(recv_ref.shape[0] // 12):
        sums[w % 4] += recv_ref[12 * w + 8 : 12 * w + 12, :]
    part_ref[...] = (sums[0] + sums[1]) + (sums[2] + sums[3])


def grads_kernel(
    off_ref, q_ref, k_ref, v_ref, pre_ref, carried_ref, att_ref, gain_ref, sums_ref,
    gq_ref, gk_ref, gv_ref, out_ref, token_ref,
):
    length, width = q_ref.shape
    inverse, _ = columns_of(sums_ref, length)
    token_ref[...] = jnp.zeros_like(token_ref)
    first, _, _ = bounds(off_ref)
    opened = row_mask(length, first=first)
    allowed = allowed_of(off_ref, length)
    for h in range(width // DH):
        query, key, value, pre = (r[:, head(h)] for r in (q_ref, k_ref, v_ref, pre_ref))
        scores = dot(query, key, 1, 1)
        weights = jnp.where(allowed, scores, 0.0).astype(BF16)
        gv_ref[:, head(h)] = dot(weights, pre, 0, 0)
        grad_scores = dot(pre, value, 1, 1)
        grad_weights = jnp.where(allowed, grad_scores, 0.0).astype(BF16)
        gk_ref[:, head(h)] = dot(grad_weights, query, 0, 0)
        out_ref[:, head(h)] = (gain_ref[:, head(h)] * (att_ref[:, head(h)] * inverse)).astype(BF16)
        carried = carried_ref[h * DH : (h + 1) * DH, :]
        carried_grad = jnp.where(opened, dot(pre, carried, 1, 1), 0.0)
        gq_ref[:, head(h)] = (dot(grad_weights, key, 1, 0) + carried_grad).astype(BF16)


def final_kernel(
    off_ref, k_ref, v_ref, later_ref, gk_ref, gv_ref, part_ref, other_ref,
    outk_ref, outv_ref, gain_ref,
):
    length, width = k_ref.shape
    _, last, _ = bounds(off_ref)
    tail = row_mask(length, last=last)
    gain_ref[...] = part_ref[...] + other_ref[...]
    for h in range(width // DH):
        later = later_ref[h * DH : (h + 1) * DH, :].astype(BF16)
        from_values = jnp.where(tail, dot(v_ref[:, head(h)], later, 1, 1), 0.0)
        from_keys = jnp.where(tail, dot(k_ref[:, head(h)], later, 1, 0), 0.0)
        outk_ref[:, head(h)] = (gk_ref[:, head(h)] + from_values).astype(BF16)
        outv_ref[:, head(h)] = (gv_ref[:, head(h)] + from_keys).astype(BF16)


def call(kernel, outs, flops, bytes_accessed, *args, ins=None, out_specs=None, scratch=(), grant=12):
    return pl.pallas_call(
        kernel,
        out_shape=[jax.ShapeDtypeStruct(s, d) for s, d in outs],
        in_specs=ins or [SMEM if a.dtype == jnp.int32 else VMEM for a in args],
        out_specs=out_specs or [VMEM] * len(outs),
        scratch_shapes=list(scratch),
        compiler_params=pltpu.CompilerParams(vmem_limit_bytes=grant << 20),
        cost_estimate=pl.CostEstimate(
            flops=flops, bytes_accessed=bytes_accessed, transcendentals=0
        ),
    )(*args)


def exchanged(rows, per):
    count = rows.shape[0] // per
    tile = {8: (8,), 9: (9, 1), 12: (3, 4)}[per]
    groups = [order_of(count)]
    moved = lax.all_to_all(
        rows.reshape((count, *tile, DH)), "seq", 0, 0, axis_index_groups=groups
    )
    return moved.reshape(rows.shape)


def shards(query, key_rows, value, gain, grad_out, start_offset):
    q, k, v, g = query[0], key_rows[0], value[0], grad_out[0]
    length, width = q.shape
    heads = width // DH
    off = start_offset
    gain = gain.reshape(1, width)
    count = lax.axis_size("seq")
    wide = (length, width)
    mega = 1 << 20
    dma = pltpu.SemaphoreType.DMA
    (tails,) = call(
        tail_kernel,
        [((count * 9, DH), F32)],
        34 * mega,
        mega,
        off,
        k,
        v,
        ins=[HBM] * 3,
        out_specs=[HBM],
        scratch=(
            pltpu.SMEM(off.shape, jnp.int32),
            pltpu.VMEM(wide, BF16),
            pltpu.VMEM(wide, BF16),
            pltpu.VMEM((count * 9, DH), F32),
            dma((3,)),
            dma((heads,)),
        ),
        grant=63,
    )
    tails = exchanged(tails, 9)
    token = (8, DH)
    local, ready = call(
        local_kernel, [(wide, F32), (token, F32)], 134 * mega, mega, off, q, k, v, gain
    )
    prefixes, keep = call(
        prefix_kernel, [((count * 8, DH), F32), ((count, DH), F32)], mega, mega, tails, ready
    )
    state = exchanged(prefixes, 8)
    att, sums, carried = call(
        attend_kernel,
        [(wide, F32), ((16, DH), F32), ((width, DH), BF16)],
        34 * mega,
        mega,
        off,
        q,
        local,
        state,
        g,
        gain,
    )
    sums = lax.all_to_all(
        sums.reshape(4, 4, DH), "tensor", 0, 0, axis_index_groups=[[2, 3, 1, 0]]
    ).reshape(16, DH)
    pre, grad_states = call(
        pre_kernel,
        [(wide, BF16), ((count * 12, DH), F32)],
        34 * mega,
        mega,
        off,
        q,
        att,
        g,
        gain,
        sums,
    )
    grad_states = exchanged(grad_states, 12)
    gq, gk, gv, out, ready = call(
        grads_kernel,
        [(wide, BF16), (wide, F32), (wide, F32), (wide, BF16), (token, F32)],
        340 * mega,
        3 * mega,
        off,
        q,
        k,
        v,
        pre,
        carried,
        att,
        gain,
        sums,
    )
    suffixes, ready = call(
        suffix_kernel,
        [((count * 8, DH), F32), (token, F32)],
        mega,
        mega,
        keep,
        grad_states,
        ready,
    )
    later = exchanged(suffixes, 8)
    (part,) = call(part_kernel, [((heads, DH), F32)], mega, mega, grad_states, ready)
    other = lax.ppermute(part, "dp", [(0, 1), (1, 0)])
    gk, gv, gain_sum = call(
        final_kernel,
        [(wide, BF16), (wide, BF16), ((heads, DH), F32)],
        68 * mega,
        2 * mega,
        off,
        k,
        v,
        later,
        gk,
        gv,
        part,
        other,
    )
    return out[None], gq[None], gk[None], gv[None], gain_sum.reshape(width)


def solution(mesh):
    wide = P("dp", "seq", "tensor")
    return jax.shard_map(
        shards,
        mesh=mesh,
        in_specs=(wide, wide, wide, P("tensor"), wide, P("dp", "seq")),
        out_specs=(wide, wide, wide, wide, P("tensor")),
        check_vma=False,
    )
```

```python
import jax
import jax.numpy as jnp
from jax import lax
from jax.experimental import pallas as pl
from jax.experimental.pallas import tpu as pltpu
from jax.sharding import PartitionSpec as P

DH = 128
BLK = 64
CH = 2048
EPS = 1e-05
ROOT = 37
VMEM = pl.BlockSpec(memory_space=pltpu.VMEM)
SMEM = pl.BlockSpec(memory_space=pltpu.SMEM)
HBM = pl.BlockSpec(memory_space=pltpu.HBM)
F32 = jnp.float32
BF16 = jnp.bfloat16


def dot(a, b, ca, cb):
    return lax.dot_general(a, b, (((ca,), (cb,)), ((), ())), preferred_element_type=F32)


def bounds(off_ref):
    first, last, count = jnp.int32(1 << 20), jnp.int32(-1), jnp.int32(0)
    for b in range(off_ref.shape[1]):
        off = off_ref[0, b]
        present = off < BLK
        first = jnp.minimum(first, jnp.where(present, b * BLK + off, 1 << 20))
        last = jnp.maximum(last, jnp.where(present, b * BLK + off, -1))
        count += present.astype(jnp.int32)
    return first, last, count


def labels_of(off_ref, pos):
    labels = jnp.zeros(pos.shape, jnp.int32)
    for b in range(off_ref.shape[1]):
        off = off_ref[0, b]
        start = jnp.where(off < BLK, b * BLK + off, 1 << 20)
        labels += (pos >= start).astype(jnp.int32)
    return labels


def allowed_of(off_ref, length):
    t = lax.broadcasted_iota(jnp.int32, (length, length), 0)
    s = lax.broadcasted_iota(jnp.int32, (length, length), 1)
    rows = labels_of(off_ref, lax.broadcasted_iota(jnp.int32, (length, 1), 0))
    cols = labels_of(off_ref, lax.broadcasted_iota(jnp.int32, (1, length), 1))
    return (rows == cols) & (s <= t)


def row_mask(length, first=None, last=None):
    pos = lax.broadcasted_iota(jnp.int32, (length, DH), 0)
    return pos < first if last is None else pos >= last


def put_slices(send_ref, h, state):
    for j in range(DH // 8):
        at = 9 * (h * (DH // 8) + j)
        send_ref[at : at + 8, :] = state[8 * j : 8 * j + 8, :]


def head(h):
    return slice(h * DH, (h + 1) * DH)


def tail_kernel(off_hbm, k_hbm, v_hbm, send_hbm, off_ref, k_ref, v_ref, send_ref, sems, sent):
    copies = [
        pltpu.make_async_copy(source, target, sems.at[i])
        for i, (source, target) in enumerate(
            ((off_hbm, off_ref), (k_hbm, k_ref), (v_hbm, v_ref))
        )
    ]
    for copy in copies:
        copy.start()
    length, width = k_ref.shape
    copies[0].wait()
    _, last, count = bounds(off_ref)
    tail = row_mask(length, last=last)
    keep = jnp.full((1, DH), jnp.where(count > 0, 0.0, 1.0), F32)
    for j in range(send_ref.shape[0] // 9):
        send_ref[9 * j + 8 : 9 * j + 9, :] = keep
    copies[1].wait()
    copies[2].wait()
    outs = []
    for h in range(width // DH):
        keys = jnp.where(tail, k_ref[:, head(h)], jnp.zeros((), BF16))
        put_slices(send_ref, h, dot(keys, v_ref[:, head(h)], 0, 0))
        rows = slice(h * 9 * (DH // 8), (h + 1) * 9 * (DH // 8))
        outs.append(pltpu.make_async_copy(send_ref.at[rows], send_hbm.at[rows], sent.at[h]))
        outs[-1].start()
    for copy in outs:
        copy.wait()


def local_kernel(off_ref, q_ref, k_ref, v_ref, gain_ref, out_ref, token_ref):
    length, width = q_ref.shape
    allowed = allowed_of(off_ref, length)
    for h in range(width // DH):
        scores = dot(q_ref[:, head(h)], k_ref[:, head(h)], 1, 1)
        weights = jnp.where(allowed, scores, 0.0).astype(BF16)
        out_ref[:, head(h)] = dot(weights, v_ref[:, head(h)], 1, 0)
    token_ref[...] = jnp.zeros_like(token_ref)


def order_of(count):
    side = 8

    def distance(w):
        steps = (abs(w // side - ROOT // side), abs(w % side - ROOT % side))
        return sum(min(d, side - d) for d in steps)

    return [ROOT] + sorted((w for w in range(count) if w != ROOT), key=lambda w: -distance(w))


def slots_of(count):
    order = order_of(count)
    return [order.index(w) for w in range(count)]


def prefix_kernel(recv_ref, token_ref, send_ref, keep_ref):
    carry = token_ref[...]
    for w in slots_of(recv_ref.shape[0] // 9):
        send_ref[8 * w : 8 * w + 8, :] = carry
        flag = recv_ref[9 * w + 8 : 9 * w + 9, :]
        keep_ref[w : w + 1, :] = flag
        carry = recv_ref[9 * w : 9 * w + 8, :] + carry * jnp.broadcast_to(flag, (8, DH))


def attend_kernel(
    off_ref, q_ref, local_ref, state_ref, g_ref, gain_ref, att_ref, sums_ref, carried_ref
):
    length, width = q_ref.shape
    first, _, _ = bounds(off_ref)
    opened = row_mask(length, first=first)
    squares = jnp.zeros((length, DH), F32)
    products = jnp.zeros((length, DH), F32)
    for h in range(width // DH):
        carried = state_ref[h * DH : (h + 1) * DH, :].astype(BF16)
        carried_ref[h * DH : (h + 1) * DH, :] = carried
        carried_out = dot(q_ref[:, head(h)], carried, 1, 0)
        att = local_ref[:, head(h)] + jnp.where(opened, carried_out, 0.0)
        att_ref[:, head(h)] = att
        squares += att * att
        products += (gain_ref[:, head(h)] * g_ref[:, head(h)].astype(F32)) * att
    row = 0
    for total in (squares, products):
        for half in range(length // DH):
            line = jnp.sum(total[half * DH : (half + 1) * DH, :].T, axis=0, keepdims=True)
            for c in range(4):
                sums_ref[4 * c + row : 4 * c + row + 1, :] = line
            row += 1


def columns_of(sums_ref, length):
    total = sums_ref[0:4, :] + sums_ref[4:8, :] + sums_ref[8:12, :] + sums_ref[12:16, :]
    halves = length // DH
    inv = lax.rsqrt(total[0:halves, :] / CH + EPS)
    mean = inv * total[halves : 2 * halves, :] / CH
    cols = jnp.concatenate([inv, mean, inv, mean], axis=0).T
    inverse = jnp.concatenate([cols[:, i : i + 1] for i in range(halves)], axis=0)
    mean = jnp.concatenate([cols[:, halves + i : halves + i + 1] for i in range(halves)], axis=0)
    return jnp.broadcast_to(inverse, (length, DH)), jnp.broadcast_to(mean, (length, DH))


def pre_kernel(off_ref, q_ref, att_ref, g_ref, gain_ref, sums_ref, pre_ref, send_ref):
    length, width = q_ref.shape
    first, _, _ = bounds(off_ref)
    opened = row_mask(length, first=first)
    inverse, mean = columns_of(sums_ref, length)
    parts = []
    for h in range(width // DH):
        normed = att_ref[:, head(h)] * inverse
        upstream = g_ref[:, head(h)].astype(F32)
        pre = inverse * (gain_ref[:, head(h)] * upstream - normed * mean)
        pre_ref[:, head(h)] = pre.astype(BF16)
        state = dot(q_ref[:, head(h)], jnp.where(opened, pre, 0.0).astype(BF16), 0, 0)
        for j in range(DH // 8):
            at = 12 * (h * (DH // 8) + j)
            send_ref[at : at + 8, :] = state[8 * j : 8 * j + 8, :]
        parts.append(jnp.sum(upstream * normed, axis=0, keepdims=True))
    part = jnp.concatenate(parts, axis=0)
    for j in range(send_ref.shape[0] // 12):
        send_ref[12 * j + 8 : 12 * j + 12, :] = part


def suffix_kernel(flags_ref, recv_ref, token_ref, send_ref, after_ref):
    carry = token_ref[...]
    after_ref[...] = carry
    for w in reversed(slots_of(recv_ref.shape[0] // 12)):
        send_ref[8 * w : 8 * w + 8, :] = carry
        keep = jnp.broadcast_to(flags_ref[w : w + 1, :], (8, DH))
        carry = recv_ref[12 * w : 12 * w + 8, :] + carry * keep


def part_kernel(recv_ref, token_ref, part_ref):
    sums = [token_ref[4 * (i % 2) : 4 * (i % 2) + 4, :] for i in range(4)]
    for w in range(recv_ref.shape[0] // 12):
        sums[w % 4] += recv_ref[12 * w + 8 : 12 * w + 12, :]
    part_ref[...] = (sums[0] + sums[1]) + (sums[2] + sums[3])


def grads_kernel(
    off_ref, q_ref, k_ref, v_ref, pre_ref, carried_ref, att_ref, gain_ref, sums_ref,
    gq_ref, gk_ref, gv_ref, out_ref, token_ref,
):
    length, width = q_ref.shape
    inverse, _ = columns_of(sums_ref, length)
    token_ref[...] = jnp.zeros_like(token_ref)
    first, _, _ = bounds(off_ref)
    opened = row_mask(length, first=first)
    allowed = allowed_of(off_ref, length)
    for h in range(width // DH):
        query, key, value, pre = (r[:, head(h)] for r in (q_ref, k_ref, v_ref, pre_ref))
        scores = dot(query, key, 1, 1)
        weights = jnp.where(allowed, scores, 0.0).astype(BF16)
        gv_ref[:, head(h)] = dot(weights, pre, 0, 0)
        grad_scores = dot(pre, value, 1, 1)
        grad_weights = jnp.where(allowed, grad_scores, 0.0).astype(BF16)
        gk_ref[:, head(h)] = dot(grad_weights, query, 0, 0)
        out_ref[:, head(h)] = (gain_ref[:, head(h)] * (att_ref[:, head(h)] * inverse)).astype(BF16)
        carried = carried_ref[h * DH : (h + 1) * DH, :]
        carried_grad = jnp.where(opened, dot(pre, carried, 1, 1), 0.0)
        gq_ref[:, head(h)] = (dot(grad_weights, key, 1, 0) + carried_grad).astype(BF16)


def final_kernel(
    off_ref, k_ref, v_ref, later_ref, gk_ref, gv_ref, part_ref, other_ref,
    outk_ref, outv_ref, gain_ref,
):
    length, width = k_ref.shape
    _, last, _ = bounds(off_ref)
    tail = row_mask(length, last=last)
    gain_ref[...] = part_ref[...] + other_ref[...]
    for h in range(width // DH):
        later = later_ref[h * DH : (h + 1) * DH, :].astype(BF16)
        from_values = jnp.where(tail, dot(v_ref[:, head(h)], later, 1, 1), 0.0)
        from_keys = jnp.where(tail, dot(k_ref[:, head(h)], later, 1, 0), 0.0)
        outk_ref[:, head(h)] = (gk_ref[:, head(h)] + from_values).astype(BF16)
        outv_ref[:, head(h)] = (gv_ref[:, head(h)] + from_keys).astype(BF16)


def call(kernel, outs, flops, bytes_accessed, *args, ins=None, out_specs=None, scratch=(), grant=12):
    return pl.pallas_call(
        kernel,
        out_shape=[jax.ShapeDtypeStruct(s, d) for s, d in outs],
        in_specs=ins or [SMEM if a.dtype == jnp.int32 else VMEM for a in args],
        out_specs=out_specs or [VMEM] * len(outs),
        scratch_shapes=list(scratch),
        compiler_params=pltpu.CompilerParams(vmem_limit_bytes=grant << 20),
        cost_estimate=pl.CostEstimate(
            flops=flops, bytes_accessed=bytes_accessed, transcendentals=0
        ),
    )(*args)


def exchanged(rows, per):
    count = rows.shape[0] // per
    tile = {8: (8,), 9: (9, 1), 12: (3, 4)}[per]
    groups = [order_of(count)]
    moved = lax.all_to_all(
        rows.reshape((count, *tile, DH)), "seq", 0, 0, axis_index_groups=groups
    )
    return moved.reshape(rows.shape)


def shards(query, key_rows, value, gain, grad_out, start_offset):
    q, k, v, g = query[0], key_rows[0], value[0], grad_out[0]
    length, width = q.shape
    heads = width // DH
    off = start_offset
    gain = gain.reshape(1, width)
    count = lax.axis_size("seq")
    wide = (length, width)
    mega = 1 << 20
    dma = pltpu.SemaphoreType.DMA
    (tails,) = call(
        tail_kernel,
        [((count * 9, DH), F32)],
        34 * mega,
        mega,
        off,
        k,
        v,
        ins=[HBM] * 3,
        out_specs=[HBM],
        scratch=(
            pltpu.SMEM(off.shape, jnp.int32),
            pltpu.VMEM(wide, BF16),
            pltpu.VMEM(wide, BF16),
            pltpu.VMEM((count * 9, DH), F32),
            dma((3,)),
            dma((heads,)),
        ),
        grant=63,
    )
    tails = exchanged(tails, 9)
    token = (8, DH)
    local, ready = call(
        local_kernel, [(wide, F32), (token, F32)], 134 * mega, mega, off, q, k, v, gain
    )
    prefixes, keep = call(
        prefix_kernel, [((count * 8, DH), F32), ((count, DH), F32)], mega, mega, tails, ready
    )
    state = exchanged(prefixes, 8)
    att, sums, carried = call(
        attend_kernel,
        [(wide, F32), ((16, DH), F32), ((width, DH), BF16)],
        34 * mega,
        mega,
        off,
        q,
        local,
        state,
        g,
        gain,
    )
    sums = lax.all_to_all(
        sums.reshape(4, 4, DH), "tensor", 0, 0, axis_index_groups=[[2, 3, 1, 0]]
    ).reshape(16, DH)
    pre, grad_states = call(
        pre_kernel,
        [(wide, BF16), ((count * 12, DH), F32)],
        34 * mega,
        mega,
        off,
        q,
        att,
        g,
        gain,
        sums,
    )
    grad_states = exchanged(grad_states, 12)
    gq, gk, gv, out, ready = call(
        grads_kernel,
        [(wide, BF16), (wide, F32), (wide, F32), (wide, BF16), (token, F32)],
        340 * mega,
        3 * mega,
        off,
        q,
        k,
        v,
        pre,
        carried,
        att,
        gain,
        sums,
    )
    suffixes, ready = call(
        suffix_kernel,
        [((count * 8, DH), F32), (token, F32)],
        mega,
        mega,
        keep,
        grad_states,
        ready,
    )
    later = exchanged(suffixes, 8)
    (part,) = call(part_kernel, [((heads, DH), F32)], mega, mega, grad_states, ready)
    other = lax.ppermute(part, "dp", [(0, 1), (1, 0)])
    gk, gv, gain_sum = call(
        final_kernel,
        [(wide, BF16), (wide, BF16), ((heads, DH), F32)],
        68 * mega,
        2 * mega,
        off,
        k,
        v,
        later,
        gk,
        gv,
        part,
        other,
    )
    return out[None], gq[None], gk[None], gv[None], gain_sum.reshape(width)


def solution(mesh):
    wide = P("dp", "seq", "tensor")
    return jax.shard_map(
        shards,
        mesh=mesh,
        in_specs=(wide, wide, wide, P("tensor"), wide, P("dp", "seq")),
        out_specs=(wide, wide, wide, wide, P("tensor")),
        check_vma=False,
    )
```

```python
import jax
import jax.numpy as jnp
from jax import lax
from jax.experimental import pallas as pl
from jax.experimental.pallas import tpu as pltpu
from jax.sharding import PartitionSpec as P

DH = 128
BLK = 64
CH = 2048
EPS = 1e-05
ROOT = 37
VMEM = pl.BlockSpec(memory_space=pltpu.VMEM)
SMEM = pl.BlockSpec(memory_space=pltpu.SMEM)
HBM = pl.BlockSpec(memory_space=pltpu.HBM)
F32 = jnp.float32
BF16 = jnp.bfloat16


def dot(a, b, ca, cb):
    return lax.dot_general(a, b, (((ca,), (cb,)), ((), ())), preferred_element_type=F32)


def bounds(off_ref):
    first, last, count = jnp.int32(1 << 20), jnp.int32(-1), jnp.int32(0)
    for b in range(off_ref.shape[1]):
        off = off_ref[0, b]
        present = off < BLK
        first = jnp.minimum(first, jnp.where(present, b * BLK + off, 1 << 20))
        last = jnp.maximum(last, jnp.where(present, b * BLK + off, -1))
        count += present.astype(jnp.int32)
    return first, last, count


def labels_of(off_ref, pos):
    labels = jnp.zeros(pos.shape, jnp.int32)
    for b in range(off_ref.shape[1]):
        off = off_ref[0, b]
        start = jnp.where(off < BLK, b * BLK + off, 1 << 20)
        labels += (pos >= start).astype(jnp.int32)
    return labels


def allowed_of(off_ref, length):
    t = lax.broadcasted_iota(jnp.int32, (length, length), 0)
    s = lax.broadcasted_iota(jnp.int32, (length, length), 1)
    rows = labels_of(off_ref, lax.broadcasted_iota(jnp.int32, (length, 1), 0))
    cols = labels_of(off_ref, lax.broadcasted_iota(jnp.int32, (1, length), 1))
    return (rows == cols) & (s <= t)


def row_mask(length, first=None, last=None):
    pos = lax.broadcasted_iota(jnp.int32, (length, DH), 0)
    return pos < first if last is None else pos >= last


def put_slices(send_ref, h, state):
    for j in range(DH // 8):
        at = 9 * (h * (DH // 8) + j)
        send_ref[at : at + 8, :] = state[8 * j : 8 * j + 8, :]


def head(h):
    return slice(h * DH, (h + 1) * DH)


def tail_kernel(off_hbm, k_hbm, v_hbm, send_hbm, off_ref, k_ref, v_ref, send_ref, sems, sent):
    copies = [
        pltpu.make_async_copy(source, target, sems.at[i])
        for i, (source, target) in enumerate(
            ((off_hbm, off_ref), (k_hbm, k_ref), (v_hbm, v_ref))
        )
    ]
    for copy in copies:
        copy.start()
    length, width = k_ref.shape
    copies[0].wait()
    _, last, count = bounds(off_ref)
    tail = row_mask(length, last=last)
    keep = jnp.full((1, DH), jnp.where(count > 0, 0.0, 1.0), F32)
    for j in range(send_ref.shape[0] // 9):
        send_ref[9 * j + 8 : 9 * j + 9, :] = keep
    copies[1].wait()
    copies[2].wait()
    outs = []
    for h in range(width // DH):
        keys = jnp.where(tail, k_ref[:, head(h)], jnp.zeros((), BF16))
        put_slices(send_ref, h, dot(keys, v_ref[:, head(h)], 0, 0))
        rows = slice(h * 9 * (DH // 8), (h + 1) * 9 * (DH // 8))
        outs.append(pltpu.make_async_copy(send_ref.at[rows], send_hbm.at[rows], sent.at[h]))
        outs[-1].start()
    for copy in outs:
        copy.wait()


def local_kernel(off_ref, q_ref, k_ref, v_ref, gain_ref, out_ref, turned_ref, token_ref):
    length, width = q_ref.shape
    first, _, _ = bounds(off_ref)
    opened = row_mask(length, first=first)
    allowed = allowed_of(off_ref, length)
    for h in range(width // DH):
        scores = dot(q_ref[:, head(h)], k_ref[:, head(h)], 1, 1)
        weights = jnp.where(allowed, scores, 0.0).astype(BF16)
        out_ref[:, head(h)] = dot(weights, v_ref[:, head(h)], 1, 0)
        query = jnp.where(opened, q_ref[:, head(h)], jnp.zeros((), BF16))
        turned_ref[h * DH : (h + 1) * DH, :] = query.T
    token_ref[...] = jnp.zeros_like(token_ref)


def order_of(count):
    side = 8

    def distance(w):
        steps = (abs(w // side - ROOT // side), abs(w % side - ROOT % side))
        return sum(min(d, side - d) for d in steps)

    return [ROOT] + sorted((w for w in range(count) if w != ROOT), key=lambda w: -distance(w))


def slots_of(count):
    order = order_of(count)
    return [order.index(w) for w in range(count)]


def prefix_kernel(recv_ref, token_ref, send_ref, keep_ref):
    carry = token_ref[...]
    for w in slots_of(recv_ref.shape[0] // 9):
        send_ref[8 * w : 8 * w + 8, :] = carry
        flag = recv_ref[9 * w + 8 : 9 * w + 9, :]
        keep_ref[w : w + 1, :] = flag
        carry = recv_ref[9 * w : 9 * w + 8, :] + carry * jnp.broadcast_to(flag, (8, DH))


def attend_kernel(
    off_ref, q_ref, local_ref, state_ref, g_ref, gain_ref, att_ref, sums_ref, carried_ref
):
    length, width = q_ref.shape
    first, _, _ = bounds(off_ref)
    opened = row_mask(length, first=first)
    squares = jnp.zeros((length, DH), F32)
    products = jnp.zeros((length, DH), F32)
    for h in range(width // DH):
        carried = state_ref[h * DH : (h + 1) * DH, :].astype(BF16)
        carried_ref[h * DH : (h + 1) * DH, :] = carried
        carried_out = dot(q_ref[:, head(h)], carried, 1, 0)
        att = local_ref[:, head(h)] + jnp.where(opened, carried_out, 0.0)
        att_ref[:, head(h)] = att
        squares += att * att
        products += (gain_ref[:, head(h)] * g_ref[:, head(h)].astype(F32)) * att
    row = 0
    for total in (squares, products):
        for half in range(length // DH):
            line = jnp.sum(total[half * DH : (half + 1) * DH, :].T, axis=0, keepdims=True)
            for c in range(4):
                sums_ref[4 * c + row : 4 * c + row + 1, :] = line
            row += 1


def columns_of(sums_ref, length):
    total = sums_ref[0:4, :] + sums_ref[4:8, :] + sums_ref[8:12, :] + sums_ref[12:16, :]
    halves = length // DH
    inv = lax.rsqrt(total[0:halves, :] / CH + EPS)
    mean = inv * total[halves : 2 * halves, :] / CH

    def column(rows):
        blocks = [jnp.broadcast_to(rows[i : i + 1], (DH, DH)).T for i in range(halves)]
        return jnp.concatenate(blocks, axis=0)

    return column(inv), column(mean)


def pre_kernel(turned_ref, att_ref, g_ref, gain_ref, sums_ref, pre_ref, send_ref):
    length, width = att_ref.shape
    inverse, mean = columns_of(sums_ref, length)
    parts = []
    for h in range(width // DH):
        normed = att_ref[:, head(h)] * inverse
        upstream = g_ref[:, head(h)].astype(F32)
        pre = inverse * (gain_ref[:, head(h)] * upstream - normed * mean)
        rounded = pre.astype(BF16)
        pre_ref[:, head(h)] = rounded
        state = dot(turned_ref[h * DH : (h + 1) * DH, :], rounded, 1, 0)
        for j in range(DH // 8):
            at = 12 * (h * (DH // 8) + j)
            send_ref[at : at + 8, :] = state[8 * j : 8 * j + 8, :]
        parts.append(jnp.sum(upstream * normed, axis=0, keepdims=True))
    part = jnp.concatenate(parts, axis=0)
    for j in range(send_ref.shape[0] // 12):
        send_ref[12 * j + 8 : 12 * j + 12, :] = part


def suffix_kernel(flags_ref, recv_ref, token_ref, send_ref, after_ref):
    carry = token_ref[...]
    after_ref[...] = carry
    for w in reversed(slots_of(recv_ref.shape[0] // 12)):
        send_ref[8 * w : 8 * w + 8, :] = carry
        keep = jnp.broadcast_to(flags_ref[w : w + 1, :], (8, DH))
        carry = recv_ref[12 * w : 12 * w + 8, :] + carry * keep


def part_kernel(recv_ref, token_ref, part_ref):
    sums = [token_ref[4 * (i % 2) : 4 * (i % 2) + 4, :] for i in range(4)]
    for w in range(recv_ref.shape[0] // 12):
        sums[w % 4] += recv_ref[12 * w + 8 : 12 * w + 12, :]
    part_ref[...] = (sums[0] + sums[1]) + (sums[2] + sums[3])


def grads_kernel(
    off_ref, q_ref, k_ref, v_ref, pre_ref, carried_ref, att_ref, gain_ref, sums_ref,
    gq_ref, gk_ref, gv_ref, out_ref, token_ref,
):
    length, width = q_ref.shape
    inverse, _ = columns_of(sums_ref, length)
    token_ref[...] = jnp.zeros_like(token_ref)
    first, _, _ = bounds(off_ref)
    opened = row_mask(length, first=first)
    allowed = allowed_of(off_ref, length)
    for h in range(width // DH):
        query, key, value, pre = (r[:, head(h)] for r in (q_ref, k_ref, v_ref, pre_ref))
        scores = dot(query, key, 1, 1)
        weights = jnp.where(allowed, scores, 0.0).astype(BF16)
        gv_ref[:, head(h)] = dot(weights, pre, 0, 0)
        grad_scores = dot(pre, value, 1, 1)
        grad_weights = jnp.where(allowed, grad_scores, 0.0).astype(BF16)
        gk_ref[:, head(h)] = dot(grad_weights, query, 0, 0)
        out_ref[:, head(h)] = (gain_ref[:, head(h)] * (att_ref[:, head(h)] * inverse)).astype(BF16)
        carried = carried_ref[h * DH : (h + 1) * DH, :]
        carried_grad = jnp.where(opened, dot(pre, carried, 1, 1), 0.0)
        gq_ref[:, head(h)] = (dot(grad_weights, key, 1, 0) + carried_grad).astype(BF16)


def final_kernel(
    off_ref, k_ref, v_ref, later_ref, gk_ref, gv_ref, part_ref, other_ref,
    outk_ref, outv_ref, gain_ref,
):
    length, width = k_ref.shape
    _, last, _ = bounds(off_ref)
    tail = row_mask(length, last=last)
    gain_ref[...] = part_ref[...] + other_ref[...]
    for h in range(width // DH):
        later = later_ref[h * DH : (h + 1) * DH, :].astype(BF16)
        from_values = jnp.where(tail, dot(v_ref[:, head(h)], later, 1, 1), 0.0)
        from_keys = jnp.where(tail, dot(k_ref[:, head(h)], later, 1, 0), 0.0)
        outk_ref[:, head(h)] = (gk_ref[:, head(h)] + from_values).astype(BF16)
        outv_ref[:, head(h)] = (gv_ref[:, head(h)] + from_keys).astype(BF16)


def call(kernel, outs, flops, bytes_accessed, *args, ins=None, out_specs=None, scratch=(), grant=12):
    return pl.pallas_call(
        kernel,
        out_shape=[jax.ShapeDtypeStruct(s, d) for s, d in outs],
        in_specs=ins or [SMEM if a.dtype == jnp.int32 else VMEM for a in args],
        out_specs=out_specs or [VMEM] * len(outs),
        scratch_shapes=list(scratch),
        compiler_params=pltpu.CompilerParams(vmem_limit_bytes=grant << 20),
        cost_estimate=pl.CostEstimate(
            flops=flops, bytes_accessed=bytes_accessed, transcendentals=0
        ),
    )(*args)


def exchanged(rows, per):
    count = rows.shape[0] // per
    tile = {8: (8,), 9: (9, 1), 12: (3, 4)}[per]
    groups = [order_of(count)]
    moved = lax.all_to_all(
        rows.reshape((count, *tile, DH)), "seq", 0, 0, axis_index_groups=groups
    )
    return moved.reshape(rows.shape)


def shards(query, key_rows, value, gain, grad_out, start_offset):
    q, k, v, g = query[0], key_rows[0], value[0], grad_out[0]
    length, width = q.shape
    heads = width // DH
    off = start_offset
    gain = gain.reshape(1, width)
    count = lax.axis_size("seq")
    wide = (length, width)
    mega = 1 << 20
    dma = pltpu.SemaphoreType.DMA
    (tails,) = call(
        tail_kernel,
        [((count * 9, DH), F32)],
        34 * mega,
        mega,
        off,
        k,
        v,
        ins=[HBM] * 3,
        out_specs=[HBM],
        scratch=(
            pltpu.SMEM(off.shape, jnp.int32),
            pltpu.VMEM(wide, BF16),
            pltpu.VMEM(wide, BF16),
            pltpu.VMEM((count * 9, DH), F32),
            dma((3,)),
            dma((heads,)),
        ),
        grant=63,
    )
    tails = exchanged(tails, 9)
    token = (8, DH)
    local, turned, ready = call(
        local_kernel,
        [(wide, F32), ((width, length), BF16), (token, F32)],
        134 * mega,
        mega,
        off,
        q,
        k,
        v,
        gain,
    )
    prefixes, keep = call(
        prefix_kernel, [((count * 8, DH), F32), ((count, DH), F32)], mega, mega, tails, ready
    )
    state = exchanged(prefixes, 8)
    att, sums, carried = call(
        attend_kernel,
        [(wide, F32), ((16, DH), F32), ((width, DH), BF16)],
        34 * mega,
        mega,
        off,
        q,
        local,
        state,
        g,
        gain,
    )
    sums = lax.all_to_all(
        sums.reshape(4, 4, DH), "tensor", 0, 0, axis_index_groups=[[2, 3, 1, 0]]
    ).reshape(16, DH)
    pre, grad_states = call(
        pre_kernel,
        [(wide, BF16), ((count * 12, DH), F32)],
        34 * mega,
        mega,
        turned,
        att,
        g,
        gain,
        sums,
    )
    grad_states = exchanged(grad_states, 12)
    gq, gk, gv, out, ready = call(
        grads_kernel,
        [(wide, BF16), (wide, F32), (wide, F32), (wide, BF16), (token, F32)],
        340 * mega,
        3 * mega,
        off,
        q,
        k,
        v,
        pre,
        carried,
        att,
        gain,
        sums,
    )
    suffixes, ready = call(
        suffix_kernel,
        [((count * 8, DH), F32), (token, F32)],
        mega,
        mega,
        keep,
        grad_states,
        ready,
    )
    later = exchanged(suffixes, 8)
    (part,) = call(part_kernel, [((heads, DH), F32)], mega, mega, grad_states, ready)
    other = lax.ppermute(part, "dp", [(0, 1), (1, 0)])
    gk, gv, gain_sum = call(
        final_kernel,
        [(wide, BF16), (wide, BF16), ((heads, DH), F32)],
        68 * mega,
        2 * mega,
        off,
        k,
        v,
        later,
        gk,
        gv,
        part,
        other,
    )
    return out[None], gq[None], gk[None], gv[None], gain_sum.reshape(width)


def solution(mesh):
    wide = P("dp", "seq", "tensor")
    return jax.shard_map(
        shards,
        mesh=mesh,
        in_specs=(wide, wide, wide, P("tensor"), wide, P("dp", "seq")),
        out_specs=(wide, wide, wide, wide, P("tensor")),
        check_vma=False,
    )
```

```python
import jax
import jax.numpy as jnp
from jax import lax
from jax.experimental import pallas as pl
from jax.experimental.pallas import tpu as pltpu
from jax.sharding import PartitionSpec as P

DH = 128
BLK = 64
CH = 2048
EPS = 1e-05
ROOT = 37
VMEM = pl.BlockSpec(memory_space=pltpu.VMEM)
SMEM = pl.BlockSpec(memory_space=pltpu.SMEM)
HBM = pl.BlockSpec(memory_space=pltpu.HBM)
F32 = jnp.float32
BF16 = jnp.bfloat16


def dot(a, b, ca, cb):
    return lax.dot_general(a, b, (((ca,), (cb,)), ((), ())), preferred_element_type=F32)


def bounds(off_ref):
    first, last, count = jnp.int32(1 << 20), jnp.int32(-1), jnp.int32(0)
    for b in range(off_ref.shape[1]):
        off = off_ref[0, b]
        present = off < BLK
        first = jnp.minimum(first, jnp.where(present, b * BLK + off, 1 << 20))
        last = jnp.maximum(last, jnp.where(present, b * BLK + off, -1))
        count += present.astype(jnp.int32)
    return first, last, count


def labels_of(off_ref, pos):
    labels = jnp.zeros(pos.shape, jnp.int32)
    for b in range(off_ref.shape[1]):
        off = off_ref[0, b]
        start = jnp.where(off < BLK, b * BLK + off, 1 << 20)
        labels += (pos >= start).astype(jnp.int32)
    return labels


def allowed_of(off_ref, length):
    t = lax.broadcasted_iota(jnp.int32, (length, length), 0)
    s = lax.broadcasted_iota(jnp.int32, (length, length), 1)
    rows = labels_of(off_ref, lax.broadcasted_iota(jnp.int32, (length, 1), 0))
    cols = labels_of(off_ref, lax.broadcasted_iota(jnp.int32, (1, length), 1))
    return (rows == cols) & (s <= t)


def row_mask(length, first=None, last=None):
    pos = lax.broadcasted_iota(jnp.int32, (length, DH), 0)
    return pos < first if last is None else pos >= last


def put_slices(send_ref, h, state):
    for j in range(DH // 8):
        at = 9 * (h * (DH // 8) + j)
        send_ref[at : at + 8, :] = state[8 * j : 8 * j + 8, :]


def head(h):
    return slice(h * DH, (h + 1) * DH)


def tail_kernel(off_hbm, k_hbm, v_hbm, send_hbm, off_ref, k_ref, v_ref, send_ref, sems, sent):
    copies = [
        pltpu.make_async_copy(source, target, sems.at[i])
        for i, (source, target) in enumerate(
            ((off_hbm, off_ref), (k_hbm, k_ref), (v_hbm, v_ref))
        )
    ]
    for copy in copies:
        copy.start()
    length, width = k_ref.shape
    copies[0].wait()
    _, last, count = bounds(off_ref)
    tail = row_mask(length, last=last)
    keep = jnp.full((1, DH), jnp.where(count > 0, 0.0, 1.0), F32)
    for j in range(send_ref.shape[0] // 9):
        send_ref[9 * j + 8 : 9 * j + 9, :] = keep
    copies[1].wait()
    copies[2].wait()
    outs = []
    for h in range(width // DH):
        keys = jnp.where(tail, k_ref[:, head(h)], jnp.zeros((), BF16))
        put_slices(send_ref, h, dot(keys, v_ref[:, head(h)], 0, 0))
        rows = slice(h * 9 * (DH // 8), (h + 1) * 9 * (DH // 8))
        outs.append(pltpu.make_async_copy(send_ref.at[rows], send_hbm.at[rows], sent.at[h]))
        outs[-1].start()
    for copy in outs:
        copy.wait()


def local_kernel(
    off_ref, q_ref, k_ref, v_ref, gain_ref, out_ref, turned_ref, open_ref, token_ref
):
    length, width = q_ref.shape
    first, _, _ = bounds(off_ref)
    opened = row_mask(length, first=first)
    open_ref[...] = jnp.where(opened, 1.0, 0.0)
    allowed = allowed_of(off_ref, length)
    for h in range(width // DH):
        scores = dot(q_ref[:, head(h)], k_ref[:, head(h)], 1, 1)
        weights = jnp.where(allowed, scores, 0.0).astype(BF16)
        out_ref[:, head(h)] = dot(weights, v_ref[:, head(h)], 1, 0)
        query = jnp.where(opened, q_ref[:, head(h)], jnp.zeros((), BF16))
        turned_ref[h * DH : (h + 1) * DH, :] = query.T
    token_ref[...] = jnp.zeros_like(token_ref)


def order_of(count):
    side = 8

    def distance(w):
        steps = (abs(w // side - ROOT // side), abs(w % side - ROOT % side))
        return sum(min(d, side - d) for d in steps)

    return [ROOT] + sorted((w for w in range(count) if w != ROOT), key=lambda w: -distance(w))


def slots_of(count):
    order = order_of(count)
    return [order.index(w) for w in range(count)]


def prefix_kernel(recv_ref, token_ref, send_ref, keep_ref):
    carry = token_ref[...]
    for w in slots_of(recv_ref.shape[0] // 9):
        send_ref[8 * w : 8 * w + 8, :] = carry
        flag = recv_ref[9 * w + 8 : 9 * w + 9, :]
        keep_ref[w : w + 1, :] = flag
        carry = recv_ref[9 * w : 9 * w + 8, :] + carry * jnp.broadcast_to(flag, (8, DH))


def attend_kernel(
    open_ref, q_ref, local_ref, state_ref, g_ref, gain_ref, att_ref, sums_ref, carried_ref
):
    length, width = q_ref.shape
    opened = open_ref[...]
    squares = jnp.zeros((length, DH), F32)
    products = jnp.zeros((length, DH), F32)
    for h in range(width // DH):
        carried = state_ref[h * DH : (h + 1) * DH, :].astype(BF16)
        carried_ref[h * DH : (h + 1) * DH, :] = carried
        carried_out = dot(q_ref[:, head(h)], carried, 1, 0)
        att = local_ref[:, head(h)] + opened * carried_out
        att_ref[:, head(h)] = att
        squares += att * att
        products += (gain_ref[:, head(h)] * g_ref[:, head(h)].astype(F32)) * att
    row = 0
    for total in (squares, products):
        for half in range(length // DH):
            line = jnp.sum(total[half * DH : (half + 1) * DH, :].T, axis=0, keepdims=True)
            for c in range(4):
                sums_ref[4 * c + row : 4 * c + row + 1, :] = line
            row += 1


def columns_of(sums_ref, length):
    total = sums_ref[0:4, :] + sums_ref[4:8, :] + sums_ref[8:12, :] + sums_ref[12:16, :]
    halves = length // DH
    inv = lax.rsqrt(total[0:halves, :] / CH + EPS)
    mean = inv * total[halves : 2 * halves, :] / CH

    def column(rows):
        blocks = [jnp.broadcast_to(rows[i : i + 1], (DH, DH)).T for i in range(halves)]
        return jnp.concatenate(blocks, axis=0)

    return column(inv), column(mean)


def pre_kernel(turned_ref, att_ref, g_ref, gain_ref, sums_ref, pre_ref, send_ref):
    length, width = att_ref.shape
    inverse, mean = columns_of(sums_ref, length)
    parts = []
    for h in range(width // DH):
        normed = att_ref[:, head(h)] * inverse
        upstream = g_ref[:, head(h)].astype(F32)
        pre = inverse * (gain_ref[:, head(h)] * upstream - normed * mean)
        rounded = pre.astype(BF16)
        pre_ref[:, head(h)] = rounded
        state = dot(turned_ref[h * DH : (h + 1) * DH, :], rounded, 1, 0)
        for j in range(DH // 8):
            at = 12 * (h * (DH // 8) + j)
            send_ref[at : at + 8, :] = state[8 * j : 8 * j + 8, :]
        parts.append(jnp.sum(upstream * normed, axis=0, keepdims=True))
    part = jnp.concatenate(parts, axis=0)
    for j in range(send_ref.shape[0] // 12):
        send_ref[12 * j + 8 : 12 * j + 12, :] = part


def suffix_kernel(flags_ref, recv_ref, token_ref, send_ref, after_ref):
    carry = token_ref[...]
    after_ref[...] = carry
    for w in reversed(slots_of(recv_ref.shape[0] // 12)):
        send_ref[8 * w : 8 * w + 8, :] = carry
        keep = jnp.broadcast_to(flags_ref[w : w + 1, :], (8, DH))
        carry = recv_ref[12 * w : 12 * w + 8, :] + carry * keep


def part_kernel(recv_ref, token_ref, part_ref):
    sums = [token_ref[4 * (i % 2) : 4 * (i % 2) + 4, :] for i in range(4)]
    for w in range(recv_ref.shape[0] // 12):
        sums[w % 4] += recv_ref[12 * w + 8 : 12 * w + 12, :]
    part_ref[...] = (sums[0] + sums[1]) + (sums[2] + sums[3])


def grads_kernel(
    off_ref, q_ref, k_ref, v_ref, pre_ref, carried_ref, att_ref, gain_ref, sums_ref,
    gq_ref, gk_ref, gv_ref, out_ref, tail_ref, token_ref,
):
    length, width = q_ref.shape
    inverse, _ = columns_of(sums_ref, length)
    token_ref[...] = jnp.zeros_like(token_ref)
    first, last, _ = bounds(off_ref)
    tail_ref[...] = jnp.where(row_mask(length, last=last), 1.0, 0.0)
    opened = row_mask(length, first=first)
    allowed = allowed_of(off_ref, length)
    for h in range(width // DH):
        query, key, value, pre = (r[:, head(h)] for r in (q_ref, k_ref, v_ref, pre_ref))
        scores = dot(query, key, 1, 1)
        weights = jnp.where(allowed, scores, 0.0).astype(BF16)
        gv_ref[:, head(h)] = dot(weights, pre, 0, 0)
        grad_scores = dot(pre, value, 1, 1)
        grad_weights = jnp.where(allowed, grad_scores, 0.0).astype(BF16)
        gk_ref[:, head(h)] = dot(grad_weights, query, 0, 0)
        out_ref[:, head(h)] = (gain_ref[:, head(h)] * (att_ref[:, head(h)] * inverse)).astype(BF16)
        carried = carried_ref[h * DH : (h + 1) * DH, :]
        carried_grad = jnp.where(opened, dot(pre, carried, 1, 1), 0.0)
        gq_ref[:, head(h)] = (dot(grad_weights, key, 1, 0) + carried_grad).astype(BF16)


def final_kernel(
    tail_ref, k_ref, v_ref, later_ref, gk_ref, gv_ref, part_ref, other_ref,
    outk_ref, outv_ref, gain_ref,
):
    width = k_ref.shape[1]
    tail = tail_ref[...]
    gain_ref[...] = part_ref[...] + other_ref[...]
    for h in range(width // DH):
        later = later_ref[h * DH : (h + 1) * DH, :].astype(BF16)
        from_values = tail * dot(v_ref[:, head(h)], later, 1, 1)
        from_keys = tail * dot(k_ref[:, head(h)], later, 1, 0)
        outk_ref[:, head(h)] = (gk_ref[:, head(h)] + from_values).astype(BF16)
        outv_ref[:, head(h)] = (gv_ref[:, head(h)] + from_keys).astype(BF16)


def call(kernel, outs, flops, bytes_accessed, *args, ins=None, out_specs=None, scratch=(), grant=12):
    return pl.pallas_call(
        kernel,
        out_shape=[jax.ShapeDtypeStruct(s, d) for s, d in outs],
        in_specs=ins or [SMEM if a.dtype == jnp.int32 else VMEM for a in args],
        out_specs=out_specs or [VMEM] * len(outs),
        scratch_shapes=list(scratch),
        compiler_params=pltpu.CompilerParams(vmem_limit_bytes=grant << 20),
        cost_estimate=pl.CostEstimate(
            flops=flops, bytes_accessed=bytes_accessed, transcendentals=0
        ),
    )(*args)


def exchanged(rows, per):
    count = rows.shape[0] // per
    tile = {8: (8,), 9: (9, 1), 12: (3, 4)}[per]
    groups = [order_of(count)]
    moved = lax.all_to_all(
        rows.reshape((count, *tile, DH)), "seq", 0, 0, axis_index_groups=groups
    )
    return moved.reshape(rows.shape)


def shards(query, key_rows, value, gain, grad_out, start_offset):
    q, k, v, g = query[0], key_rows[0], value[0], grad_out[0]
    length, width = q.shape
    heads = width // DH
    off = start_offset
    gain = gain.reshape(1, width)
    count = lax.axis_size("seq")
    wide = (length, width)
    mega = 1 << 20
    dma = pltpu.SemaphoreType.DMA
    (tails,) = call(
        tail_kernel,
        [((count * 9, DH), F32)],
        34 * mega,
        mega,
        off,
        k,
        v,
        ins=[HBM] * 3,
        out_specs=[HBM],
        scratch=(
            pltpu.SMEM(off.shape, jnp.int32),
            pltpu.VMEM(wide, BF16),
            pltpu.VMEM(wide, BF16),
            pltpu.VMEM((count * 9, DH), F32),
            dma((3,)),
            dma((heads,)),
        ),
        grant=63,
    )
    tails = exchanged(tails, 9)
    token = (8, DH)
    local, turned, opened, ready = call(
        local_kernel,
        [(wide, F32), ((width, length), BF16), ((length, DH), F32), (token, F32)],
        134 * mega,
        mega,
        off,
        q,
        k,
        v,
        gain,
    )
    prefixes, keep = call(
        prefix_kernel, [((count * 8, DH), F32), ((count, DH), F32)], mega, mega, tails, ready
    )
    state = exchanged(prefixes, 8)
    att, sums, carried = call(
        attend_kernel,
        [(wide, F32), ((16, DH), F32), ((width, DH), BF16)],
        34 * mega,
        mega,
        opened,
        q,
        local,
        state,
        g,
        gain,
    )
    sums = lax.all_to_all(
        sums.reshape(4, 4, DH), "tensor", 0, 0, axis_index_groups=[[2, 3, 1, 0]]
    ).reshape(16, DH)
    pre, grad_states = call(
        pre_kernel,
        [(wide, BF16), ((count * 12, DH), F32)],
        34 * mega,
        mega,
        turned,
        att,
        g,
        gain,
        sums,
    )
    grad_states = exchanged(grad_states, 12)
    gq, gk, gv, out, tail, ready = call(
        grads_kernel,
        [
            (wide, BF16),
            (wide, F32),
            (wide, F32),
            (wide, BF16),
            ((length, DH), F32),
            (token, F32),
        ],
        340 * mega,
        3 * mega,
        off,
        q,
        k,
        v,
        pre,
        carried,
        att,
        gain,
        sums,
    )
    suffixes, ready = call(
        suffix_kernel,
        [((count * 8, DH), F32), (token, F32)],
        mega,
        mega,
        keep,
        grad_states,
        ready,
    )
    later = exchanged(suffixes, 8)
    (part,) = call(part_kernel, [((heads, DH), F32)], mega, mega, grad_states, ready)
    other = lax.ppermute(part, "dp", [(0, 1), (1, 0)])
    gk, gv, gain_sum = call(
        final_kernel,
        [(wide, BF16), (wide, BF16), ((heads, DH), F32)],
        68 * mega,
        2 * mega,
        tail,
        k,
        v,
        later,
        gk,
        gv,
        part,
        other,
    )
    return out[None], gq[None], gk[None], gv[None], gain_sum.reshape(width)


def solution(mesh):
    wide = P("dp", "seq", "tensor")
    return jax.shard_map(
        shards,
        mesh=mesh,
        in_specs=(wide, wide, wide, P("tensor"), wide, P("dp", "seq")),
        out_specs=(wide, wide, wide, wide, P("tensor")),
        check_vma=False,
    )
```
